256 devices in a mesh: seq: 8 (over z_lo, x), tensor: 32 (over z_hi, y, core).
Axes of the slice: x: 4, y: 4, z: 8 (z_hi: 4, z_lo: 2; z = z_hi * 2 + z_lo), core: 2. Of those that a mesh axis runs over, the one named last changes fastest.
Arguments:
- tokens: bfloat16 [768, 8192], P('tensor', 'seq'), may hold values from -6 to 6
- w_gate: bfloat16 [8192, 28672], P('seq', 'tensor'), may hold values from -0.109375 to 0.109375
- w_up: bfloat16 [8192, 28672], P('seq', 'tensor'), may hold values from -0.109375 to 0.109375
- w_down: bfloat16 [28672, 8192], P('tensor', 'seq'), may hold values from -0.0546875 to 0.0546875
- mask_gate: int32 [64, 224], P('seq', 'tensor'), may hold values 0 or 1
- mask_up: int32 [64, 224], P('seq', 'tensor'), may hold values 0 or 1
- mask_down: int32 [224, 64], P('tensor', 'seq'), may hold values 0 or 1
- cotangent: bfloat16 [768, 8192], P('tensor', 'seq'), may hold values from -6 to 6
Outputs:
- output: bfloat16 [768, 8192], P('tensor', 'seq')
- grad_tokens: bfloat16 [768, 8192], P('tensor', 'seq')
- grad_gate: bfloat16 [8192, 28672], P('seq', 'tensor')
- grad_up: bfloat16 [8192, 28672], P('seq', 'tensor')
- grad_down: bfloat16 [28672, 8192], P('tensor', 'seq')
The draws below stay inside these ranges and needn't reach their ends.
All inputs are finite; a program needn't handle non-finite values. No bound on the sum of `mask_gate` or of `mask_up` or of `mask_down` on one device may be relied on, other than what follows from the above.
Results may differ from the reference program's by a relative error of at most 0.0049.
Values may be sent and summed in bfloat16 or wider, within the bound.
A program may use at most 128 MiB of HBM per device.

```python
import jax
import jax.numpy as jnp

D = 8192
FF = 28672
BLK = 128
TOKENS = 768


def set_ends(result, rng, least, high):
    dims = result.shape
    index_at = [jax.random.randint(jax.random.fold_in(rng, axis), (), 0, dims[axis]) for axis in range(len(dims))]
    result = result.at[tuple(index_at)].set(least)
    longest = dims.index(max(dims))
    index_at[longest] = (index_at[longest] + 1) % dims[longest]
    return result.at[tuple(index_at)].set(high)


def block_levels(own_key, shape, shards, low, largest):
    def one(dim, parts):
        heights = jax.random.uniform(jax.random.fold_in(jax.random.fold_in(own_key, 6), dim), (parts,), jnp.float32, low / len(shards), largest / len(shards))
        return jnp.repeat(jnp.exp(heights), shape[dim] // parts).reshape((-1,) + (1,) * (len(shape) - dim - 1))

    loudness = one(*shards[0])
    for cut in shards[1:]:
        loudness = loudness * one(*cut)
    return loudness


def bell_draw(own_key, dims, scale, most, cuts=(), held_as=jnp.bfloat16):
    gain = block_levels(own_key, dims, cuts, -0.22, 0.18) if cuts else 1.0
    array = jax.random.normal(own_key, dims, jnp.float32) * scale * gain
    return jnp.minimum(jnp.maximum(array, -most), most).astype(held_as)


def setup_inputs(seed: int = 0) -> dict:
    key_of = jax.random.split(jax.random.key(seed), 9)
    return {
        "tokens": bell_draw(key_of[0], (TOKENS, D), 1.0, 6.0, ((0, 32), (1, 8))),
        "w_gate": bell_draw(key_of[1], (D, FF), (2 * D // 5) ** -0.5, 0.109375, ((0, 8), (1, 32))),
        "w_up": bell_draw(key_of[2], (D, FF), (2 * D // 5) ** -0.5, 0.109375, ((0, 8), (1, 32))),
        "w_down": bell_draw(key_of[3], (FF, D), (2 * FF // 5) ** -0.5, 0.0546875, ((0, 32), (1, 8))),
        "mask_gate": set_ends((jax.random.randint(key_of[4], (D // BLK, FF // BLK), 0, 5) < 2).astype(jnp.int32), jax.random.fold_in(key_of[4], 1), 0, 1),
        "mask_up": set_ends((jax.random.randint(key_of[5], (D // BLK, FF // BLK), 0, 5) < 2).astype(jnp.int32), jax.random.fold_in(key_of[5], 1), 0, 1),
        "mask_down": set_ends((jax.random.randint(key_of[6], (FF // BLK, D // BLK), 0, 5) < 2).astype(jnp.int32), jax.random.fold_in(key_of[6], 1), 0, 1),
        "cotangent": bell_draw(key_of[7], (TOKENS, D), 1.0, 6.0, ((0, 32), (1, 8))),
    }


def widen(mask):
    full = jnp.repeat(jnp.repeat(mask, BLK, axis=0), BLK, axis=1)
    return full.astype(jnp.bfloat16)


def reference(tokens, w_gate, w_up, w_down, mask_gate, mask_up, mask_down, cotangent):
    gate_mask = widen(mask_gate)
    up_mask = widen(mask_up)
    down_mask = widen(mask_down)
    gate_w = w_gate * gate_mask
    up_w = w_up * up_mask
    down_w = w_down * down_mask
    gate = jnp.dot(tokens, gate_w, preferred_element_type=jnp.float32)
    up = jnp.dot(tokens, up_w, preferred_element_type=jnp.float32)
    sig = jax.nn.sigmoid(gate)
    act = gate * sig
    hidden = (act * up).astype(jnp.bfloat16)
    output = jnp.dot(hidden, down_w, preferred_element_type=jnp.float32).astype(jnp.bfloat16)
    grad_hidden = jnp.dot(cotangent, down_w.T, preferred_element_type=jnp.float32)
    dgate = (grad_hidden * up * sig * (1.0 + gate * (1.0 - sig))).astype(jnp.bfloat16)
    dup = (grad_hidden * act).astype(jnp.bfloat16)
    grad_tokens = (jnp.dot(dgate, gate_w.T, preferred_element_type=jnp.float32)
                   + jnp.dot(dup, up_w.T, preferred_element_type=jnp.float32)).astype(jnp.bfloat16)
    grad_gate = (jnp.dot(tokens.T, dgate, preferred_element_type=jnp.float32) * gate_mask).astype(jnp.bfloat16)
    grad_up = (jnp.dot(tokens.T, dup, preferred_element_type=jnp.float32) * up_mask).astype(jnp.bfloat16)
    grad_down = (jnp.dot(hidden.T, cotangent, preferred_element_type=jnp.float32) * down_mask).astype(jnp.bfloat16)
    return output, grad_tokens, grad_gate, grad_up, grad_down
```

```python
import jax
import jax.numpy as jnp
from jax import lax
from jax.sharding import PartitionSpec as P


def widen(mask, rows):
    block = rows // mask.shape[0]
    full = jnp.repeat(jnp.repeat(mask, block, axis=0), block, axis=1)
    return full.astype(jnp.bfloat16)


def gating(summed, width):
    gate = summed[:, :width]
    up = summed[:, width:]
    sig = jax.nn.sigmoid(gate)
    act = gate * sig
    return (gate, up, sig, act)


def gate_up_grads(gate, up, sig, act, grad_hidden):
    dgate = (grad_hidden * up * sig * (1.0 + gate * (1.0 - sig))).astype(jnp.bfloat16)
    dup = (grad_hidden * act).astype(jnp.bfloat16)
    return jnp.concatenate([dgate, dup], axis=1)


def per_device(tokens, w_gate, w_up, w_down, mask_gate, mask_up, mask_down, cotangent):
    width = w_gate.shape[1]
    feat = tokens.shape[1]
    gate_mask = widen(mask_gate, w_gate.shape[0])
    up_mask = widen(mask_up, w_up.shape[0])
    down_mask = widen(mask_down, w_down.shape[0])
    joined = jnp.concatenate([w_gate * gate_mask, w_up * up_mask], axis=1)
    down_w = w_down * down_mask
    contract_first = (((0,), (0,)), ((), ()))
    contract_last = (((1,), (1,)), ((), ()))
    both = lax.all_gather(
        jnp.concatenate([tokens, cotangent], axis=1), "tensor", axis=0, tiled=True
    )
    gathered = both[:, :feat]
    cot_rows = both[:, feat:]
    partial_value = jnp.dot(gathered, joined, preferred_element_type=jnp.float32)
    summed = lax.psum_scatter(partial_value, "seq", scatter_dimension=0, tiled=True)
    gate, up, sig, act = gating(summed, width)
    hidden_part = (act * up).astype(jnp.bfloat16)
    hidden = lax.all_gather(hidden_part, "seq", axis=0, tiled=True)
    output = lax.psum_scatter(
        jnp.dot(hidden, down_w, preferred_element_type=jnp.float32),
        "tensor",
        scatter_dimension=0,
        tiled=True,
    ).astype(jnp.bfloat16)
    grad_part = lax.dot_general(cot_rows, down_w, contract_last, preferred_element_type=jnp.float32)
    grad_hidden = lax.psum_scatter(grad_part, "seq", scatter_dimension=0, tiled=True)
    grads_part = gate_up_grads(gate, up, sig, act, grad_hidden)
    grads = lax.all_gather(grads_part, "seq", axis=0, tiled=True)
    grad_tokens = lax.psum_scatter(
        lax.dot_general(grads, joined, contract_last, preferred_element_type=jnp.float32),
        "tensor",
        scatter_dimension=0,
        tiled=True,
    ).astype(jnp.bfloat16)
    weight_grad = lax.dot_general(
        gathered, grads, contract_first, preferred_element_type=jnp.float32
    )
    grad_gate = (weight_grad[:, :width] * gate_mask).astype(jnp.bfloat16)
    grad_up = (weight_grad[:, width:] * up_mask).astype(jnp.bfloat16)
    down_grad = lax.dot_general(
        hidden, cot_rows, contract_first, preferred_element_type=jnp.float32
    )
    grad_down = (down_grad * down_mask).astype(jnp.bfloat16)
    return (output, grad_tokens, grad_gate, grad_up, grad_down)


def solution(mesh):
    return jax.shard_map(
        per_device,
        mesh=mesh,
        in_specs=(
            P("tensor", "seq"),
            P("seq", "tensor"),
            P("seq", "tensor"),
            P("tensor", "seq"),
            P("seq", "tensor"),
            P("seq", "tensor"),
            P("tensor", "seq"),
            P("tensor", "seq"),
        ),
        out_specs=(
            P("tensor", "seq"),
            P("tensor", "seq"),
            P("seq", "tensor"),
            P("seq", "tensor"),
            P("tensor", "seq"),
        ),
        check_vma=False,
    )
```

```python
import functools

import jax
import jax.numpy as jnp
from jax import lax
from jax.experimental import pallas as pl
from jax.experimental.pallas import tpu as pltpu
from jax.sharding import PartitionSpec as P

MESH = pl.DeviceIdType.MESH
AXES = ("seq", "tensor")


def peer(axis, j):
    return tuple(j if a == axis else lax.axis_index(a) for a in AXES)


def exchange_kernel(axis, n, gather, x_ref, y_ref, send_sem, recv_sem, own_sem):
    me = lax.axis_index(axis)
    barrier = pltpu.get_barrier_semaphore()

    def greet(k, carry):
        j = lax.rem(me + k, n)
        pl.semaphore_signal(barrier, inc=1, device_id=peer(axis, j), device_id_type=MESH)
        return carry

    lax.fori_loop(1, n, greet, 0)
    pl.semaphore_wait(barrier, n - 1)

    def src(j):
        return x_ref if gather else x_ref.at[j]

    def remote(j, slot):
        return pltpu.make_async_remote_copy(
            src_ref=src(j),
            dst_ref=y_ref.at[slot],
            send_sem=send_sem.at[j],
            recv_sem=recv_sem.at[slot],
            device_id=peer(axis, j),
            device_id_type=MESH,
        )

    own = pltpu.make_async_copy(src(me), y_ref.at[me], own_sem)
    own.start()

    def send(k, carry):
        remote(lax.rem(me + k, n), me).start()
        return carry

    lax.fori_loop(1, n, send, 0)

    def finish(k, carry):
        remote(lax.rem(me + k, n), me).wait_send()
        i = lax.rem(me + n - k, n)
        remote(i, i).wait_recv()
        return carry

    lax.fori_loop(1, n, finish, 0)
    own.wait()


def exchange(x, axis, n, gather, cid):
    shape = (n,) + x.shape if gather else x.shape
    return pl.pallas_call(
        functools.partial(exchange_kernel, axis, n, gather),
        out_shape=jax.ShapeDtypeStruct(shape, x.dtype),
        in_specs=[pl.BlockSpec(memory_space=pl.ANY)],
        out_specs=pl.BlockSpec(memory_space=pl.ANY),
        scratch_shapes=[
            pltpu.SemaphoreType.DMA((n,)),
            pltpu.SemaphoreType.DMA((n,)),
            pltpu.SemaphoreType.DMA,
        ],
        compiler_params=pltpu.CompilerParams(collective_id=cid, has_side_effects=True),
    )(x)


def gather_rows(x, axis, n, cid):
    y = exchange(x, axis, n, True, cid)
    return y.reshape((n * x.shape[0],) + x.shape[1:])


def sum_scatter_rows(x, axis, n, cid):
    rows = x.shape[0] // n
    y = exchange(x.reshape((n, rows) + x.shape[1:]), axis, n, False, cid)
    return jnp.sum(y, axis=0)


def widen(mask, rows):
    block = rows // mask.shape[0]
    full = jnp.repeat(jnp.repeat(mask, block, axis=0), block, axis=1)
    return full.astype(jnp.bfloat16)


def gating(summed, width):
    gate = summed[:, :width]
    up = summed[:, width:]
    sig = jax.nn.sigmoid(gate)
    act = gate * sig
    return (gate, up, sig, act)


def gate_up_grads(gate, up, sig, act, grad_hidden):
    dgate = (grad_hidden * up * sig * (1.0 + gate * (1.0 - sig))).astype(jnp.bfloat16)
    dup = (grad_hidden * act).astype(jnp.bfloat16)
    return jnp.concatenate([dgate, dup], axis=1)


def per_device(nseq, ntensor, tokens, w_gate, w_up, w_down, mask_gate, mask_up, mask_down, cotangent):
    width = w_gate.shape[1]
    feat = tokens.shape[1]
    gate_mask = widen(mask_gate, w_gate.shape[0])
    up_mask = widen(mask_up, w_up.shape[0])
    down_mask = widen(mask_down, w_down.shape[0])
    joined = jnp.concatenate([w_gate * gate_mask, w_up * up_mask], axis=1)
    down_w = w_down * down_mask
    contract_first = (((0,), (0,)), ((), ()))
    contract_last = (((1,), (1,)), ((), ()))
    both = gather_rows(jnp.concatenate([tokens, cotangent], axis=1), "tensor", ntensor, 0)
    gathered = both[:, :feat]
    cot_rows = both[:, feat:]
    partial_value = jnp.dot(gathered, joined, preferred_element_type=jnp.float32)
    summed = lax.psum_scatter(partial_value, "seq", scatter_dimension=0, tiled=True)
    gate, up, sig, act = gating(summed, width)
    hidden_part = (act * up).astype(jnp.bfloat16)
    hidden = lax.all_gather(hidden_part, "seq", axis=0, tiled=True)
    output = sum_scatter_rows(
        jnp.dot(hidden, down_w, preferred_element_type=jnp.float32), "tensor", ntensor, 1
    ).astype(jnp.bfloat16)
    grad_part = lax.dot_general(cot_rows, down_w, contract_last, preferred_element_type=jnp.float32)
    grad_hidden = lax.psum_scatter(grad_part, "seq", scatter_dimension=0, tiled=True)
    grads_part = gate_up_grads(gate, up, sig, act, grad_hidden)
    grads = lax.all_gather(grads_part, "seq", axis=0, tiled=True)
    grad_tokens = sum_scatter_rows(
        lax.dot_general(grads, joined, contract_last, preferred_element_type=jnp.float32),
        "tensor",
        ntensor,
        2,
    ).astype(jnp.bfloat16)
    weight_grad = lax.dot_general(
        gathered, grads, contract_first, preferred_element_type=jnp.float32
    )
    grad_gate = (weight_grad[:, :width] * gate_mask).astype(jnp.bfloat16)
    grad_up = (weight_grad[:, width:] * up_mask).astype(jnp.bfloat16)
    down_grad = lax.dot_general(
        hidden, cot_rows, contract_first, preferred_element_type=jnp.float32
    )
    grad_down = (down_grad * down_mask).astype(jnp.bfloat16)
    return (output, grad_tokens, grad_gate, grad_up, grad_down)


def solution(mesh):
    return jax.shard_map(
        functools.partial(per_device, mesh.shape["seq"], mesh.shape["tensor"]),
        mesh=mesh,
        in_specs=(
            P("tensor", "seq"),
            P("seq", "tensor"),
            P("seq", "tensor"),
            P("tensor", "seq"),
            P("seq", "tensor"),
            P("seq", "tensor"),
            P("tensor", "seq"),
            P("tensor", "seq"),
        ),
        out_specs=(
            P("tensor", "seq"),
            P("tensor", "seq"),
            P("seq", "tensor"),
            P("seq", "tensor"),
            P("tensor", "seq"),
        ),
        check_vma=False,
    )
```

```python
import functools

import jax
import numpy as np
import jax.numpy as jnp
from jax import lax
from jax.experimental import pallas as pl
from jax.experimental.pallas import tpu as pltpu
from jax.sharding import PartitionSpec as P

MESH = pl.DeviceIdType.MESH
AXES = ("seq", "tensor")


def peer(axis, j):
    return tuple(j if a == axis else lax.axis_index(a) for a in AXES)


def exchange_kernel(axis, n, stride, gather, x_ref, y_ref, send_sem, recv_sem, own_sem):
    index = lax.axis_index(axis)
    me = lax.rem(index // stride, n)
    base = index - me * stride
    barrier = pltpu.get_barrier_semaphore()

    def device(j):
        return peer(axis, base + j * stride)

    def greet(k, carry):
        j = lax.rem(me + k, n)
        pl.semaphore_signal(barrier, inc=1, device_id=device(j), device_id_type=MESH)
        return carry

    lax.fori_loop(1, n, greet, 0)
    pl.semaphore_wait(barrier, n - 1)

    def src(j):
        return x_ref if gather else x_ref.at[j]

    def remote(j, slot):
        return pltpu.make_async_remote_copy(
            src_ref=src(j),
            dst_ref=y_ref.at[slot],
            send_sem=send_sem.at[j],
            recv_sem=recv_sem.at[slot],
            device_id=device(j),
            device_id_type=MESH,
        )

    own = pltpu.make_async_copy(src(me), y_ref.at[me], own_sem)
    own.start()

    def send(k, carry):
        remote(lax.rem(me + k, n), me).start()
        return carry

    lax.fori_loop(1, n, send, 0)

    def finish(k, carry):
        remote(lax.rem(me + k, n), me).wait_send()
        i = lax.rem(me + n - k, n)
        remote(i, i).wait_recv()
        return carry

    lax.fori_loop(1, n, finish, 0)
    own.wait()


class Ids:
    def __init__(self):
        self.next = 0

    def take(self):
        self.next += 1
        return self.next - 1


def exchange(x, axis, n, stride, gather, cid):
    shape = (n,) + x.shape if gather else x.shape
    return pl.pallas_call(
        functools.partial(exchange_kernel, axis, n, stride, gather),
        out_shape=jax.ShapeDtypeStruct(shape, x.dtype),
        in_specs=[pl.BlockSpec(memory_space=pl.ANY)],
        out_specs=pl.BlockSpec(memory_space=pl.ANY),
        scratch_shapes=[
            pltpu.SemaphoreType.DMA((n,)),
            pltpu.SemaphoreType.DMA((n,)),
            pltpu.SemaphoreType.DMA,
        ],
        compiler_params=pltpu.CompilerParams(collective_id=cid, has_side_effects=True),
    )(x)


def gather_rows(x, axis, digits, ids):
    for n, stride in digits:
        x = exchange(x, axis, n, stride, True, ids.take())
    return x.reshape((-1,) + x.shape[-1:])


def sum_scatter_rows(x, axis, digits, ids):
    for n, stride in reversed(digits):
        x = x.reshape((n, -1) + x.shape[-1:])
        x = jnp.sum(exchange(x, axis, n, stride, False, ids.take()), axis=0)
    return x


def widen(mask, rows):
    block = rows // mask.shape[0]
    full = jnp.repeat(jnp.repeat(mask, block, axis=0), block, axis=1)
    return full.astype(jnp.bfloat16)


def gating(summed, width):
    gate = summed[:, :width]
    up = summed[:, width:]
    sig = jax.nn.sigmoid(gate)
    act = gate * sig
    return (gate, up, sig, act)


def gate_up_grads(gate, up, sig, act, grad_hidden):
    dgate = (grad_hidden * up * sig * (1.0 + gate * (1.0 - sig))).astype(jnp.bfloat16)
    dup = (grad_hidden * act).astype(jnp.bfloat16)
    return jnp.concatenate([dgate, dup], axis=1)


def per_device(tensor_digits, tokens, w_gate, w_up, w_down, mask_gate, mask_up, mask_down, cotangent):
    width = w_gate.shape[1]
    feat = tokens.shape[1]
    gate_mask = widen(mask_gate, w_gate.shape[0])
    up_mask = widen(mask_up, w_up.shape[0])
    down_mask = widen(mask_down, w_down.shape[0])
    joined = jnp.concatenate([w_gate * gate_mask, w_up * up_mask], axis=1)
    down_w = w_down * down_mask
    contract_first = (((0,), (0,)), ((), ()))
    contract_last = (((1,), (1,)), ((), ()))
    ids = Ids()
    both = gather_rows(jnp.concatenate([tokens, cotangent], axis=1), "tensor", tensor_digits, ids)
    gathered = both[:, :feat]
    cot_rows = both[:, feat:]
    partial_value = jnp.dot(gathered, joined, preferred_element_type=jnp.float32)
    summed = lax.psum_scatter(partial_value, "seq", scatter_dimension=0, tiled=True)
    gate, up, sig, act = gating(summed, width)
    hidden_part = (act * up).astype(jnp.bfloat16)
    hidden = lax.all_gather(hidden_part, "seq", axis=0, tiled=True)
    output = sum_scatter_rows(
        jnp.dot(hidden, down_w, preferred_element_type=jnp.float32), "tensor", tensor_digits, ids
    ).astype(jnp.bfloat16)
    grad_part = lax.dot_general(cot_rows, down_w, contract_last, preferred_element_type=jnp.float32)
    grad_hidden = lax.psum_scatter(grad_part, "seq", scatter_dimension=0, tiled=True)
    grads_part = gate_up_grads(gate, up, sig, act, grad_hidden)
    grads = lax.all_gather(grads_part, "seq", axis=0, tiled=True)
    grad_tokens = sum_scatter_rows(
        lax.dot_general(grads, joined, contract_last, preferred_element_type=jnp.float32),
        "tensor",
        tensor_digits,
        ids,
    ).astype(jnp.bfloat16)
    weight_grad = lax.dot_general(
        gathered, grads, contract_first, preferred_element_type=jnp.float32
    )
    grad_gate = (weight_grad[:, :width] * gate_mask).astype(jnp.bfloat16)
    grad_up = (weight_grad[:, width:] * up_mask).astype(jnp.bfloat16)
    down_grad = lax.dot_general(
        hidden, cot_rows, contract_first, preferred_element_type=jnp.float32
    )
    grad_down = (down_grad * down_mask).astype(jnp.bfloat16)
    return (output, grad_tokens, grad_gate, grad_up, grad_down)


def axis_parts(mesh, axis):
    n = mesh.shape[axis]
    line = np.moveaxis(mesh.devices, mesh.axis_names.index(axis), -1).reshape(-1, n)[0]
    try:
        keys = [tuple(d.coords) + (d.core_on_chip,) for d in line]
    except AttributeError:
        return [n]
    parts, stride = [], 1
    while stride < n:
        changed = [c for c in range(len(keys[0])) if keys[stride][c] != keys[0][c]]
        size = 1
        while stride * size < n:
            moved = [c for c in range(len(keys[0])) if keys[stride * size][c] != keys[0][c]]
            if moved != changed:
                break
            size += 1
        if (n // stride) % size:
            return [n]
        parts.append(size)
        stride *= size
    return parts[::-1]


def digits_of(mesh, axis):
    sizes = axis_parts(mesh, axis)
    digits, stride = [], 1
    for n in reversed(sizes):
        if n > 1:
            digits.append((n, stride))
        stride *= n
    return tuple(reversed(digits))


def solution(mesh):
    return jax.shard_map(
        functools.partial(per_device, digits_of(mesh, "tensor")),
        mesh=mesh,
        in_specs=(
            P("tensor", "seq"),
            P("seq", "tensor"),
            P("seq", "tensor"),
            P("tensor", "seq"),
            P("seq", "tensor"),
            P("seq", "tensor"),
            P("tensor", "seq"),
            P("tensor", "seq"),
        ),
        out_specs=(
            P("tensor", "seq"),
            P("tensor", "seq"),
            P("seq", "tensor"),
            P("seq", "tensor"),
            P("tensor", "seq"),
        ),
        check_vma=False,
    )
```

```python
import functools

import jax
import numpy as np
import jax.numpy as jnp
from jax import lax
from jax.experimental import pallas as pl
from jax.experimental.pallas import tpu as pltpu
from jax.sharding import PartitionSpec as P

MESH = pl.DeviceIdType.MESH
AXES = ("seq", "tensor")


def peer(axis, j):
    return tuple(j if a == axis else lax.axis_index(a) for a in AXES)


def exchange_kernel(axis, n, stride, gather, x_ref, y_ref, send_sem, recv_sem):
    index = lax.axis_index(axis)
    me = lax.rem(index // stride, n)
    base = index - me * stride
    barrier = pltpu.get_barrier_semaphore()

    def device(j):
        return peer(axis, base + j * stride)

    def greet(k, carry):
        pl.semaphore_signal(
            barrier, inc=1, device_id=device(lax.rem(me + k, n)), device_id_type=MESH
        )
        return carry

    lax.fori_loop(1, n, greet, 0)
    pl.semaphore_wait(barrier, n - 1)

    def remote(k, direction):
        return pltpu.make_async_remote_copy(
            src_ref=x_ref if gather else x_ref.at[k],
            dst_ref=y_ref.at[k - 1],
            send_sem=send_sem.at[k - 1],
            recv_sem=recv_sem.at[k - 1],
            device_id=device(lax.rem(me + direction * k + n, n)),
            device_id_type=MESH,
        )

    ahead = -1 if gather else 1

    def send(k, carry):
        remote(k, ahead).start()
        return carry

    lax.fori_loop(1, n, send, 0)

    def finish(k, carry):
        remote(k, ahead).wait_send()
        remote(k, -ahead).wait_recv()
        return carry

    lax.fori_loop(1, n, finish, 0)


class Ids:
    def __init__(self):
        self.next = 0

    def take(self):
        self.next += 1
        return self.next - 1


def exchange(x, axis, n, stride, gather, cid):
    shape = (n - 1,) + (x.shape if gather else x.shape[1:])
    return pl.pallas_call(
        functools.partial(exchange_kernel, axis, n, stride, gather),
        out_shape=jax.ShapeDtypeStruct(shape, x.dtype),
        in_specs=[pl.BlockSpec(memory_space=pl.ANY)],
        out_specs=pl.BlockSpec(memory_space=pl.ANY),
        scratch_shapes=[
            pltpu.SemaphoreType.DMA((n - 1,)),
            pltpu.SemaphoreType.DMA((n - 1,)),
        ],
        compiler_params=pltpu.CompilerParams(collective_id=cid, has_side_effects=True),
    )(x)


def gather_rows(x, axis, digits, ids):
    for n, stride in digits:
        x = jnp.concatenate([x[None], exchange(x, axis, n, stride, True, ids.take())])
    return x.reshape((-1,) + x.shape[-1:])


def sum_scatter_rows(x, axis, digits, ids):
    for n, stride in reversed(digits):
        x = x.reshape((n, -1) + x.shape[-1:])
        x = x[0] + jnp.sum(exchange(x, axis, n, stride, False, ids.take()), axis=0)
    return x


def widen(mask, rows):
    block = rows // mask.shape[0]
    full = jnp.repeat(jnp.repeat(mask, block, axis=0), block, axis=1)
    return full.astype(jnp.bfloat16)


def gating(summed, width):
    gate = summed[:, :width]
    up = summed[:, width:]
    sig = jax.nn.sigmoid(gate)
    act = gate * sig
    return (gate, up, sig, act)


def gate_up_grads(gate, up, sig, act, grad_hidden):
    dgate = (grad_hidden * up * sig * (1.0 + gate * (1.0 - sig))).astype(jnp.bfloat16)
    dup = (grad_hidden * act).astype(jnp.bfloat16)
    return jnp.concatenate([dgate, dup], axis=1)


def per_device(tensor_digits, tokens, w_gate, w_up, w_down, mask_gate, mask_up, mask_down, cotangent):
    width = w_gate.shape[1]
    feat = tokens.shape[1]
    gate_mask = widen(mask_gate, w_gate.shape[0])
    up_mask = widen(mask_up, w_up.shape[0])
    down_mask = widen(mask_down, w_down.shape[0])
    joined = jnp.concatenate([w_gate * gate_mask, w_up * up_mask], axis=1)
    down_w = w_down * down_mask
    contract_first = (((0,), (0,)), ((), ()))
    contract_last = (((1,), (1,)), ((), ()))
    ids = Ids()
    both = gather_rows(jnp.concatenate([tokens, cotangent], axis=1), "tensor", tensor_digits, ids)
    gathered = both[:, :feat]
    cot_rows = both[:, feat:]
    partial_value = jnp.dot(gathered, joined, preferred_element_type=jnp.float32)
    summed = lax.psum_scatter(partial_value, "seq", scatter_dimension=0, tiled=True)
    gate, up, sig, act = gating(summed, width)
    hidden_part = (act * up).astype(jnp.bfloat16)
    hidden = lax.all_gather(hidden_part, "seq", axis=0, tiled=True)
    output = sum_scatter_rows(
        jnp.dot(hidden, down_w, preferred_element_type=jnp.float32), "tensor", tensor_digits, ids
    ).astype(jnp.bfloat16)
    grad_part = lax.dot_general(cot_rows, down_w, contract_last, preferred_element_type=jnp.float32)
    grad_hidden = lax.psum_scatter(grad_part, "seq", scatter_dimension=0, tiled=True)
    grads_part = gate_up_grads(gate, up, sig, act, grad_hidden)
    grads = lax.all_gather(grads_part, "seq", axis=0, tiled=True)
    grad_tokens = sum_scatter_rows(
        lax.dot_general(grads, joined, contract_last, preferred_element_type=jnp.float32),
        "tensor",
        tensor_digits,
        ids,
    ).astype(jnp.bfloat16)
    weight_grad = lax.dot_general(
        gathered, grads, contract_first, preferred_element_type=jnp.float32
    )
    grad_gate = (weight_grad[:, :width] * gate_mask).astype(jnp.bfloat16)
    grad_up = (weight_grad[:, width:] * up_mask).astype(jnp.bfloat16)
    down_grad = lax.dot_general(
        hidden, cot_rows, contract_first, preferred_element_type=jnp.float32
    )
    grad_down = (down_grad * down_mask).astype(jnp.bfloat16)
    return (output, grad_tokens, grad_gate, grad_up, grad_down)


def axis_parts(mesh, axis):
    n = mesh.shape[axis]
    line = np.moveaxis(mesh.devices, mesh.axis_names.index(axis), -1).reshape(-1, n)[0]
    try:
        keys = [tuple(d.coords) + (d.core_on_chip,) for d in line]
    except AttributeError:
        return [n]
    parts, stride = [], 1
    while stride < n:
        changed = [c for c in range(len(keys[0])) if keys[stride][c] != keys[0][c]]
        size = 1
        while stride * size < n:
            moved = [c for c in range(len(keys[0])) if keys[stride * size][c] != keys[0][c]]
            if moved != changed:
                break
            size += 1
        if (n // stride) % size:
            return [n]
        parts.append(size)
        stride *= size
    return parts[::-1]


def digits_of(mesh, axis):
    sizes = axis_parts(mesh, axis)
    digits, stride = [], 1
    for n in reversed(sizes):
        if n > 1:
            digits.append((n, stride))
        stride *= n
    return tuple(reversed(digits))


def solution(mesh):
    return jax.shard_map(
        functools.partial(per_device, digits_of(mesh, "tensor")),
        mesh=mesh,
        in_specs=(
            P("tensor", "seq"),
            P("seq", "tensor"),
            P("seq", "tensor"),
            P("tensor", "seq"),
            P("seq", "tensor"),
            P("seq", "tensor"),
            P("tensor", "seq"),
            P("tensor", "seq"),
        ),
        out_specs=(
            P("tensor", "seq"),
            P("tensor", "seq"),
            P("seq", "tensor"),
            P("seq", "tensor"),
            P("tensor", "seq"),
        ),
        check_vma=False,
    )
```

```python
import functools

import jax
import numpy as np
import jax.numpy as jnp
from jax import lax
from jax.experimental import pallas as pl
from jax.experimental.pallas import tpu as pltpu
from jax.sharding import PartitionSpec as P

MESH = pl.DeviceIdType.MESH
AXES = ("seq", "tensor")


def peer(axis, j):
    return tuple(j if a == axis else lax.axis_index(a) for a in AXES)


def exchange_kernel(axis, n, stride, gather, absolute, x_ref, y_ref, send_sem, recv_sem):
    index = lax.axis_index(axis)
    me = lax.rem(index // stride, n)
    base = index - me * stride
    barrier = pltpu.get_barrier_semaphore()

    def device(j):
        return peer(axis, base + j * stride)

    def greet(k, carry):
        pl.semaphore_signal(
            barrier, inc=1, device_id=device(lax.rem(me + k, n)), device_id_type=MESH
        )
        return carry

    lax.fori_loop(1, n, greet, 0)
    pl.semaphore_wait(barrier, n - 1)

    def remote(k, direction):
        other = lax.rem(me + direction * k + n, n)
        if absolute and gather:
            slot = me if direction == ahead else other
        else:
            slot = k - 1
        return pltpu.make_async_remote_copy(
            src_ref=x_ref if gather else x_ref.at[other if absolute else k],
            dst_ref=y_ref.at[slot],
            send_sem=send_sem.at[k - 1],
            recv_sem=recv_sem.at[slot],
            device_id=device(other),
            device_id_type=MESH,
        )

    ahead = 1 if absolute or not gather else -1

    def send(k, carry):
        remote(k, ahead).start()
        return carry

    lax.fori_loop(1, n, send, 0)

    def finish(k, carry):
        remote(k, ahead).wait_send()
        remote(k, -ahead).wait_recv()
        return carry

    lax.fori_loop(1, n, finish, 0)


class Ids:
    def __init__(self):
        self.next = 0

    def take(self):
        self.next += 1
        return self.next - 1


def exchange(x, axis, n, stride, gather, cid, absolute=False):
    slots = n if absolute and gather else n - 1
    shape = (slots,) + (x.shape if gather else x.shape[1:])
    return pl.pallas_call(
        functools.partial(exchange_kernel, axis, n, stride, gather, absolute),
        out_shape=jax.ShapeDtypeStruct(shape, x.dtype),
        in_specs=[pl.BlockSpec(memory_space=pl.ANY)],
        out_specs=pl.BlockSpec(memory_space=pl.ANY),
        scratch_shapes=[
            pltpu.SemaphoreType.DMA((n - 1,)),
            pltpu.SemaphoreType.DMA((slots,)),
        ],
        compiler_params=pltpu.CompilerParams(collective_id=cid, has_side_effects=True),
    )(x)


def gather_rows(x, axis, digits, ids):
    for n, stride in digits:
        x = jnp.concatenate([x[None], exchange(x, axis, n, stride, True, ids.take())])
    return x.reshape((-1,) + x.shape[-1:])


def sum_scatter_rows(x, axis, digits, ids):
    for n, stride in reversed(digits):
        x = x.reshape((n, -1) + x.shape[-1:])
        x = x[0] + jnp.sum(exchange(x, axis, n, stride, False, ids.take()), axis=0)
    return x


def digit(axis, n, stride):
    return lax.rem(lax.axis_index(axis) // stride, n)


def gather_rows_absolute(x, axis, digits, ids):
    for n, stride in digits:
        y = exchange(x, axis, n, stride, True, ids.take(), absolute=True)
        x = lax.dynamic_update_index_in_dim(y, x, digit(axis, n, stride), 0)
    return x.reshape((-1,) + x.shape[-1:])


def sum_scatter_rows_absolute(x, axis, digits, ids):
    for n, stride in reversed(digits):
        x = x.reshape((n, -1) + x.shape[-1:])
        own = lax.dynamic_index_in_dim(x, digit(axis, n, stride), 0, keepdims=False)
        x = own + jnp.sum(exchange(x, axis, n, stride, False, ids.take(), absolute=True), axis=0)
    return x


def widen(mask, rows):
    block = rows // mask.shape[0]
    full = jnp.repeat(jnp.repeat(mask, block, axis=0), block, axis=1)
    return full.astype(jnp.bfloat16)


def gating(summed, width):
    gate = summed[:, :width]
    up = summed[:, width:]
    sig = jax.nn.sigmoid(gate)
    act = gate * sig
    return (gate, up, sig, act)


def gate_up_grads(gate, up, sig, act, grad_hidden):
    dgate = (grad_hidden * up * sig * (1.0 + gate * (1.0 - sig))).astype(jnp.bfloat16)
    dup = (grad_hidden * act).astype(jnp.bfloat16)
    return jnp.concatenate([dgate, dup], axis=1)


def per_device(tensor_digits, seq_digits, tokens, w_gate, w_up, w_down, mask_gate, mask_up, mask_down, cotangent):
    width = w_gate.shape[1]
    feat = tokens.shape[1]
    gate_mask = widen(mask_gate, w_gate.shape[0])
    up_mask = widen(mask_up, w_up.shape[0])
    down_mask = widen(mask_down, w_down.shape[0])
    joined = jnp.concatenate([w_gate * gate_mask, w_up * up_mask], axis=1)
    down_w = w_down * down_mask
    contract_first = (((0,), (0,)), ((), ()))
    contract_last = (((1,), (1,)), ((), ()))
    ids = Ids()
    both = gather_rows(jnp.concatenate([tokens, cotangent], axis=1), "tensor", tensor_digits, ids)
    gathered = both[:, :feat]
    cot_rows = both[:, feat:]
    partial_value = jnp.dot(gathered, joined, preferred_element_type=jnp.float32)
    summed = sum_scatter_rows_absolute(partial_value, "seq", seq_digits, ids)
    gate, up, sig, act = gating(summed, width)
    hidden_part = (act * up).astype(jnp.bfloat16)
    hidden = gather_rows_absolute(hidden_part, "seq", seq_digits, ids)
    output = sum_scatter_rows(
        jnp.dot(hidden, down_w, preferred_element_type=jnp.float32), "tensor", tensor_digits, ids
    ).astype(jnp.bfloat16)
    grad_part = lax.dot_general(cot_rows, down_w, contract_last, preferred_element_type=jnp.float32)
    grad_hidden = sum_scatter_rows_absolute(grad_part, "seq", seq_digits, ids)
    grads_part = gate_up_grads(gate, up, sig, act, grad_hidden)
    grads = gather_rows_absolute(grads_part, "seq", seq_digits, ids)
    grad_tokens = sum_scatter_rows(
        lax.dot_general(grads, joined, contract_last, preferred_element_type=jnp.float32),
        "tensor",
        tensor_digits,
        ids,
    ).astype(jnp.bfloat16)
    weight_grad = lax.dot_general(
        gathered, grads, contract_first, preferred_element_type=jnp.float32
    )
    grad_gate = (weight_grad[:, :width] * gate_mask).astype(jnp.bfloat16)
    grad_up = (weight_grad[:, width:] * up_mask).astype(jnp.bfloat16)
    down_grad = lax.dot_general(
        hidden, cot_rows, contract_first, preferred_element_type=jnp.float32
    )
    grad_down = (down_grad * down_mask).astype(jnp.bfloat16)
    return (output, grad_tokens, grad_gate, grad_up, grad_down)


def axis_parts(mesh, axis):
    n = mesh.shape[axis]
    line = np.moveaxis(mesh.devices, mesh.axis_names.index(axis), -1).reshape(-1, n)[0]
    try:
        keys = [tuple(d.coords) + (d.core_on_chip,) for d in line]
    except AttributeError:
        return [n]
    parts, stride = [], 1
    while stride < n:
        changed = [c for c in range(len(keys[0])) if keys[stride][c] != keys[0][c]]
        size = 1
        while stride * size < n:
            moved = [c for c in range(len(keys[0])) if keys[stride * size][c] != keys[0][c]]
            if moved != changed:
                break
            size += 1
        if (n // stride) % size:
            return [n]
        parts.append(size)
        stride *= size
    return parts[::-1]


def digits_of(mesh, axis):
    sizes = axis_parts(mesh, axis)
    digits, stride = [], 1
    for n in reversed(sizes):
        if n > 1:
            digits.append((n, stride))
        stride *= n
    return tuple(reversed(digits))


def solution(mesh):
    return jax.shard_map(
        functools.partial(per_device, digits_of(mesh, "tensor"), digits_of(mesh, "seq")),
        mesh=mesh,
        in_specs=(
            P("tensor", "seq"),
            P("seq", "tensor"),
            P("seq", "tensor"),
            P("tensor", "seq"),
            P("seq", "tensor"),
            P("seq", "tensor"),
            P("tensor", "seq"),
            P("tensor", "seq"),
        ),
        out_specs=(
            P("tensor", "seq"),
            P("tensor", "seq"),
            P("seq", "tensor"),
            P("seq", "tensor"),
            P("tensor", "seq"),
        ),
        check_vma=False,
    )
```

```python
import functools

import jax
import numpy as np
import jax.numpy as jnp
from jax import lax
from jax.experimental import pallas as pl
from jax.experimental.pallas import tpu as pltpu
from jax.sharding import PartitionSpec as P

MESH = pl.DeviceIdType.MESH
AXES = ("seq", "tensor")


def peer(axis, j):
    return tuple(j if a == axis else lax.axis_index(a) for a in AXES)


def exchange_kernel(axis, n, stride, gather, absolute, x_ref, y_ref, send_sem, recv_sem):
    index = lax.axis_index(axis)
    me = lax.rem(index // stride, n)
    base = index - me * stride
    barrier = pltpu.get_barrier_semaphore()

    def device(j):
        return peer(axis, base + j * stride)

    def greet(k, carry):
        pl.semaphore_signal(
            barrier, inc=1, device_id=device(lax.rem(me + k, n)), device_id_type=MESH
        )
        return carry

    lax.fori_loop(1, n, greet, 0)
    pl.semaphore_wait(barrier, n - 1)

    def remote(k, direction):
        other = lax.rem(me + direction * k + n, n)
        if absolute and gather:
            slot = me if direction == ahead else other
        else:
            slot = k - 1
        return pltpu.make_async_remote_copy(
            src_ref=x_ref if gather else x_ref.at[other if absolute else k],
            dst_ref=y_ref.at[slot],
            send_sem=send_sem.at[k - 1],
            recv_sem=recv_sem.at[slot],
            device_id=device(other),
            device_id_type=MESH,
        )

    ahead = 1 if absolute or not gather else -1

    def send(k, carry):
        remote(k, ahead).start()
        return carry

    lax.fori_loop(1, n, send, 0)

    def finish(k, carry):
        remote(k, ahead).wait_send()
        remote(k, -ahead).wait_recv()
        return carry

    lax.fori_loop(1, n, finish, 0)


class Ids:
    def __init__(self):
        self.next = 0

    def take(self):
        self.next += 1
        return self.next - 1


def exchange(x, axis, n, stride, gather, cid, absolute=False):
    slots = n if absolute and gather else n - 1
    shape = (slots,) + (x.shape if gather else x.shape[1:])
    return pl.pallas_call(
        functools.partial(exchange_kernel, axis, n, stride, gather, absolute),
        out_shape=jax.ShapeDtypeStruct(shape, x.dtype),
        in_specs=[pl.BlockSpec(memory_space=pl.ANY)],
        out_specs=pl.BlockSpec(memory_space=pl.ANY),
        scratch_shapes=[
            pltpu.SemaphoreType.DMA((n - 1,)),
            pltpu.SemaphoreType.DMA((slots,)),
        ],
        compiler_params=pltpu.CompilerParams(collective_id=cid, has_side_effects=True),
    )(x)


def gather_rows(x, axis, digits, ids):
    for n, stride in digits:
        x = jnp.concatenate([x[None], exchange(x, axis, n, stride, True, ids.take())])
    return x.reshape((-1,) + x.shape[-1:])


def sum_scatter_rows(x, axis, digits, ids):
    for n, stride in reversed(digits):
        x = x.reshape((n, -1) + x.shape[-1:])
        x = x[0] + jnp.sum(exchange(x, axis, n, stride, False, ids.take()), axis=0)
    return x


def digit(axis, n, stride):
    return lax.rem(lax.axis_index(axis) // stride, n)


def gather_rows_absolute(x, axis, digits, ids):
    for n, stride in digits:
        y = exchange(x, axis, n, stride, True, ids.take(), absolute=True)
        x = lax.dynamic_update_index_in_dim(y, x, digit(axis, n, stride), 0)
    return x.reshape((-1,) + x.shape[-1:])


def sum_scatter_rows_absolute(x, axis, digits, ids):
    for n, stride in reversed(digits):
        x = x.reshape((n, -1) + x.shape[-1:])
        own = lax.dynamic_index_in_dim(x, digit(axis, n, stride), 0, keepdims=False)
        x = own + jnp.sum(exchange(x, axis, n, stride, False, ids.take(), absolute=True), axis=0)
    return x


def reorder_blocks(x, sizes):
    k = len(sizes)
    x = x.reshape(tuple(sizes) + (-1, x.shape[-1]))
    x = jnp.transpose(x, tuple(reversed(range(k))) + (k, k + 1))
    return x.reshape((-1, x.shape[-1]))


def seq_sum_scatter(x, digits, ids):
    x = reorder_blocks(x, [n for n, _ in digits])
    return sum_scatter_rows_absolute(x, "seq", digits, ids)


def seq_gather(x, digits, ids):
    x = gather_rows_absolute(x, "seq", digits, ids)
    return reorder_blocks(x, [n for n, _ in reversed(digits)])


def widen(mask, rows):
    block = rows // mask.shape[0]
    full = jnp.repeat(jnp.repeat(mask, block, axis=0), block, axis=1)
    return full.astype(jnp.bfloat16)


def gating(summed, width):
    gate = summed[:, :width]
    up = summed[:, width:]
    sig = jax.nn.sigmoid(gate)
    act = gate * sig
    return (gate, up, sig, act)


def gate_up_grads(gate, up, sig, act, grad_hidden):
    dgate = (grad_hidden * up * sig * (1.0 + gate * (1.0 - sig))).astype(jnp.bfloat16)
    dup = (grad_hidden * act).astype(jnp.bfloat16)
    return jnp.concatenate([dgate, dup], axis=1)


def per_device(tensor_digits, seq_digits, tokens, w_gate, w_up, w_down, mask_gate, mask_up, mask_down, cotangent):
    width = w_gate.shape[1]
    feat = tokens.shape[1]
    gate_mask = widen(mask_gate, w_gate.shape[0])
    up_mask = widen(mask_up, w_up.shape[0])
    down_mask = widen(mask_down, w_down.shape[0])
    joined = jnp.concatenate([w_gate * gate_mask, w_up * up_mask], axis=1)
    down_w = w_down * down_mask
    contract_first = (((0,), (0,)), ((), ()))
    contract_last = (((1,), (1,)), ((), ()))
    ids = Ids()
    both = gather_rows(jnp.concatenate([tokens, cotangent], axis=1), "tensor", tensor_digits, ids)
    gathered = both[:, :feat]
    cot_rows = both[:, feat:]
    partial_value = jnp.dot(gathered, joined, preferred_element_type=jnp.float32)
    summed = lax.psum_scatter(partial_value, "seq", scatter_dimension=0, tiled=True)
    gate, up, sig, act = gating(summed, width)
    hidden_part = (act * up).astype(jnp.bfloat16)
    hidden = seq_gather(hidden_part, seq_digits, ids)
    output = sum_scatter_rows(
        jnp.dot(hidden, down_w, preferred_element_type=jnp.float32), "tensor", tensor_digits, ids
    ).astype(jnp.bfloat16)
    grad_part = lax.dot_general(cot_rows, down_w, contract_last, preferred_element_type=jnp.float32)
    grad_hidden = seq_sum_scatter(grad_part, seq_digits, ids)
    grads_part = gate_up_grads(gate, up, sig, act, grad_hidden)
    grads = lax.all_gather(grads_part, "seq", axis=0, tiled=True)
    grad_tokens = sum_scatter_rows(
        lax.dot_general(grads, joined, contract_last, preferred_element_type=jnp.float32),
        "tensor",
        tensor_digits,
        ids,
    ).astype(jnp.bfloat16)
    weight_grad = lax.dot_general(
        gathered, grads, contract_first, preferred_element_type=jnp.float32
    )
    grad_gate = (weight_grad[:, :width] * gate_mask).astype(jnp.bfloat16)
    grad_up = (weight_grad[:, width:] * up_mask).astype(jnp.bfloat16)
    down_grad = lax.dot_general(
        hidden, cot_rows, contract_first, preferred_element_type=jnp.float32
    )
    grad_down = (down_grad * down_mask).astype(jnp.bfloat16)
    return (output, grad_tokens, grad_gate, grad_up, grad_down)


def axis_parts(mesh, axis):
    n = mesh.shape[axis]
    line = np.moveaxis(mesh.devices, mesh.axis_names.index(axis), -1).reshape(-1, n)[0]
    try:
        keys = [tuple(d.coords) + (d.core_on_chip,) for d in line]
    except AttributeError:
        return [n]
    parts, stride = [], 1
    while stride < n:
        changed = [c for c in range(len(keys[0])) if keys[stride][c] != keys[0][c]]
        size = 1
        while stride * size < n:
            moved = [c for c in range(len(keys[0])) if keys[stride * size][c] != keys[0][c]]
            if moved != changed:
                break
            size += 1
        if (n // stride) % size:
            return [n]
        parts.append(size)
        stride *= size
    return parts[::-1]


def digits_of(mesh, axis):
    sizes = axis_parts(mesh, axis)
    digits, stride = [], 1
    for n in reversed(sizes):
        if n > 1:
            digits.append((n, stride))
        stride *= n
    return tuple(reversed(digits))


def solution(mesh):
    return jax.shard_map(
        functools.partial(per_device, digits_of(mesh, "tensor"), digits_of(mesh, "seq")),
        mesh=mesh,
        in_specs=(
            P("tensor", "seq"),
            P("seq", "tensor"),
            P("seq", "tensor"),
            P("tensor", "seq"),
            P("seq", "tensor"),
            P("seq", "tensor"),
            P("tensor", "seq"),
            P("tensor", "seq"),
        ),
        out_specs=(
            P("tensor", "seq"),
            P("tensor", "seq"),
            P("seq", "tensor"),
            P("seq", "tensor"),
            P("tensor", "seq"),
        ),
        check_vma=False,
    )
```

```python
import functools

import jax
import numpy as np
import jax.numpy as jnp
from jax import lax
from jax.experimental import pallas as pl
from jax.experimental.pallas import tpu as pltpu
from jax.sharding import PartitionSpec as P

MESH = pl.DeviceIdType.MESH
AXES = ("seq", "tensor")


def peer(axis, j):
    return tuple(j if a == axis else lax.axis_index(a) for a in AXES)


def exchange_kernel(axis, n, stride, gather, absolute, x_ref, y_ref, send_sem, recv_sem):
    index = lax.axis_index(axis)
    me = lax.rem(index // stride, n)
    base = index - me * stride
    barrier = pltpu.get_barrier_semaphore()

    def device(j):
        return peer(axis, base + j * stride)

    def greet(k, carry):
        pl.semaphore_signal(
            barrier, inc=1, device_id=device(lax.rem(me + k, n)), device_id_type=MESH
        )
        return carry

    lax.fori_loop(1, n, greet, 0)
    pl.semaphore_wait(barrier, n - 1)

    def remote(k, direction):
        other = lax.rem(me + direction * k + n, n)
        if absolute and gather:
            slot = me if direction == ahead else other
        else:
            slot = k - 1
        return pltpu.make_async_remote_copy(
            src_ref=x_ref if gather else x_ref.at[other if absolute else k],
            dst_ref=y_ref.at[slot],
            send_sem=send_sem.at[k - 1],
            recv_sem=recv_sem.at[slot],
            device_id=device(other),
            device_id_type=MESH,
        )

    ahead = 1 if absolute or not gather else -1

    def send(k, carry):
        remote(k, ahead).start()
        return carry

    lax.fori_loop(1, n, send, 0)

    def finish(k, carry):
        remote(k, ahead).wait_send()
        remote(k, -ahead).wait_recv()
        return carry

    lax.fori_loop(1, n, finish, 0)


class Ids:
    def __init__(self):
        self.next = 0

    def take(self):
        self.next += 1
        return self.next - 1


def exchange(x, axis, n, stride, gather, cid, absolute=False):
    slots = n if absolute and gather else n - 1
    shape = (slots,) + (x.shape if gather else x.shape[1:])
    return pl.pallas_call(
        functools.partial(exchange_kernel, axis, n, stride, gather, absolute),
        out_shape=jax.ShapeDtypeStruct(shape, x.dtype),
        in_specs=[pl.BlockSpec(memory_space=pl.ANY)],
        out_specs=pl.BlockSpec(memory_space=pl.ANY),
        scratch_shapes=[
            pltpu.SemaphoreType.DMA((n - 1,)),
            pltpu.SemaphoreType.DMA((slots,)),
        ],
        compiler_params=pltpu.CompilerParams(collective_id=cid, has_side_effects=True),
    )(x)


def gather_rows(x, axis, digits, ids):
    for n, stride in digits:
        x = jnp.concatenate([x[None], exchange(x, axis, n, stride, True, ids.take())])
    return x.reshape((-1,) + x.shape[-1:])


def sum_scatter_rows(x, axis, digits, ids):
    for n, stride in reversed(digits):
        x = x.reshape((n, -1) + x.shape[-1:])
        x = x[0] + jnp.sum(exchange(x, axis, n, stride, False, ids.take()), axis=0)
    return x


def digit(axis, n, stride):
    return lax.rem(lax.axis_index(axis) // stride, n)


def gather_rows_absolute(x, axis, digits, ids):
    for n, stride in digits:
        y = exchange(x, axis, n, stride, True, ids.take(), absolute=True)
        x = lax.dynamic_update_index_in_dim(y, x, digit(axis, n, stride), 0)
    return x.reshape((-1,) + x.shape[-1:])


def sum_scatter_rows_absolute(x, axis, digits, ids):
    for n, stride in reversed(digits):
        x = x.reshape((n, -1) + x.shape[-1:])
        own = lax.dynamic_index_in_dim(x, digit(axis, n, stride), 0, keepdims=False)
        x = own + jnp.sum(exchange(x, axis, n, stride, False, ids.take(), absolute=True), axis=0)
    return x


def reorder_blocks(x, sizes):
    k = len(sizes)
    x = x.reshape(tuple(sizes) + (-1, x.shape[-1]))
    x = jnp.transpose(x, tuple(reversed(range(k))) + (k, k + 1))
    return x.reshape((-1, x.shape[-1]))


def seq_sum_scatter(x, digits, ids):
    x = reorder_blocks(x, [n for n, _ in digits])
    return sum_scatter_rows_absolute(x, "seq", digits, ids)


def seq_gather(x, digits, ids):
    x = gather_rows_absolute(x, "seq", digits, ids)
    return reorder_blocks(x, [n for n, _ in reversed(digits)])


def widen(mask, rows):
    block = rows // mask.shape[0]
    full = jnp.repeat(jnp.repeat(mask, block, axis=0), block, axis=1)
    return full.astype(jnp.bfloat16)


def gating(summed, width):
    gate = summed[:, :width]
    up = summed[:, width:]
    sig = jax.nn.sigmoid(gate)
    act = gate * sig
    return (gate, up, sig, act)


def gate_up_grads(gate, up, sig, act, grad_hidden):
    dgate = (grad_hidden * up * sig * (1.0 + gate * (1.0 - sig))).astype(jnp.bfloat16)
    dup = (grad_hidden * act).astype(jnp.bfloat16)
    return jnp.concatenate([dgate, dup], axis=1)


def per_device(tensor_digits, seq_digits, tokens, w_gate, w_up, w_down, mask_gate, mask_up, mask_down, cotangent):
    width = w_gate.shape[1]
    feat = tokens.shape[1]
    gate_mask = widen(mask_gate, w_gate.shape[0])
    up_mask = widen(mask_up, w_up.shape[0])
    down_mask = widen(mask_down, w_down.shape[0])
    joined = jnp.concatenate([w_gate * gate_mask, w_up * up_mask], axis=1)
    down_w = w_down * down_mask
    contract_first = (((0,), (0,)), ((), ()))
    contract_last = (((1,), (1,)), ((), ()))
    ids = Ids()
    both = gather_rows(jnp.concatenate([tokens, cotangent], axis=1), "tensor", tensor_digits, ids)
    gathered = both[:, :feat]
    cot_rows = both[:, feat:]
    partial_value = jnp.dot(gathered, joined, preferred_element_type=jnp.float32)
    summed = lax.psum_scatter(partial_value, "seq", scatter_dimension=0, tiled=True)
    gate, up, sig, act = gating(summed, width)
    hidden_part = (act * up).astype(jnp.bfloat16)
    hidden = seq_gather(hidden_part, seq_digits, ids)
    output = sum_scatter_rows(
        jnp.dot(hidden, down_w, preferred_element_type=jnp.float32), "tensor", tensor_digits, ids
    ).astype(jnp.bfloat16)
    grad_part = lax.dot_general(cot_rows, down_w, contract_last, preferred_element_type=jnp.float32)
    grad_hidden = lax.psum_scatter(grad_part, "seq", scatter_dimension=0, tiled=True)
    grads_part = gate_up_grads(gate, up, sig, act, grad_hidden)
    grads_part, hidden = lax.optimization_barrier((grads_part, hidden))
    grads = lax.all_gather(grads_part, "seq", axis=0, tiled=True)
    grad_tokens = sum_scatter_rows(
        lax.dot_general(grads, joined, contract_last, preferred_element_type=jnp.float32),
        "tensor",
        tensor_digits,
        ids,
    ).astype(jnp.bfloat16)
    weight_grad = lax.dot_general(
        gathered, grads, contract_first, preferred_element_type=jnp.float32
    )
    grad_gate = (weight_grad[:, :width] * gate_mask).astype(jnp.bfloat16)
    grad_up = (weight_grad[:, width:] * up_mask).astype(jnp.bfloat16)
    down_grad = lax.dot_general(
        hidden, cot_rows, contract_first, preferred_element_type=jnp.float32
    )
    grad_down = (down_grad * down_mask).astype(jnp.bfloat16)
    return (output, grad_tokens, grad_gate, grad_up, grad_down)


def axis_parts(mesh, axis):
    n = mesh.shape[axis]
    line = np.moveaxis(mesh.devices, mesh.axis_names.index(axis), -1).reshape(-1, n)[0]
    try:
        keys = [tuple(d.coords) + (d.core_on_chip,) for d in line]
    except AttributeError:
        return [n]
    parts, stride = [], 1
    while stride < n:
        changed = [c for c in range(len(keys[0])) if keys[stride][c] != keys[0][c]]
        size = 1
        while stride * size < n:
            moved = [c for c in range(len(keys[0])) if keys[stride * size][c] != keys[0][c]]
            if moved != changed:
                break
            size += 1
        if (n // stride) % size:
            return [n]
        parts.append(size)
        stride *= size
    return parts[::-1]


def digits_of(mesh, axis):
    sizes = axis_parts(mesh, axis)
    digits, stride = [], 1
    for n in reversed(sizes):
        if n > 1:
            digits.append((n, stride))
        stride *= n
    return tuple(reversed(digits))


def solution(mesh):
    return jax.shard_map(
        functools.partial(per_device, digits_of(mesh, "tensor"), digits_of(mesh, "seq")),
        mesh=mesh,
        in_specs=(
            P("tensor", "seq"),
            P("seq", "tensor"),
            P("seq", "tensor"),
            P("tensor", "seq"),
            P("seq", "tensor"),
            P("seq", "tensor"),
            P("tensor", "seq"),
            P("tensor", "seq"),
        ),
        out_specs=(
            P("tensor", "seq"),
            P("tensor", "seq"),
            P("seq", "tensor"),
            P("seq", "tensor"),
            P("tensor", "seq"),
        ),
        check_vma=False,
    )
```

```python
import functools

import jax
import numpy as np
import jax.numpy as jnp
from jax import lax
from jax.experimental import pallas as pl
from jax.experimental.pallas import tpu as pltpu
from jax.sharding import PartitionSpec as P

MESH = pl.DeviceIdType.MESH
AXES = ("seq", "tensor")


def peer(axis, j):
    return tuple(j if a == axis else lax.axis_index(a) for a in AXES)


def exchange_kernel(axis, n, stride, gather, absolute, x_ref, y_ref, send_sem, recv_sem):
    index = lax.axis_index(axis)
    me = lax.rem(index // stride, n)
    base = index - me * stride
    barrier = pltpu.get_barrier_semaphore()

    def device(j):
        return peer(axis, base + j * stride)

    def greet(k, carry):
        pl.semaphore_signal(
            barrier, inc=1, device_id=device(lax.rem(me + k, n)), device_id_type=MESH
        )
        return carry

    lax.fori_loop(1, n, greet, 0)
    pl.semaphore_wait(barrier, n - 1)

    def remote(k, direction):
        other = lax.rem(me + direction * k + n, n)
        if absolute and gather:
            slot = me if direction == ahead else other
        else:
            slot = k - 1
        return pltpu.make_async_remote_copy(
            src_ref=x_ref if gather else x_ref.at[other if absolute else k],
            dst_ref=y_ref.at[slot],
            send_sem=send_sem.at[k - 1],
            recv_sem=recv_sem.at[slot],
            device_id=device(other),
            device_id_type=MESH,
        )

    ahead = 1 if absolute or not gather else -1

    def send(k, carry):
        remote(k, ahead).start()
        return carry

    lax.fori_loop(1, n, send, 0)

    def finish(k, carry):
        remote(k, ahead).wait_send()
        remote(k, -ahead).wait_recv()
        return carry

    lax.fori_loop(1, n, finish, 0)


def multi_sum_kernel(axis, groups, *refs):
    m = len(groups)
    x_refs, y_refs, sems = refs[:m], refs[m:2 * m], refs[2 * m:]
    index = lax.axis_index(axis)
    barrier = pltpu.get_barrier_semaphore()
    infos = []
    for n, stride in groups:
        me = lax.rem(index // stride, n)
        infos.append((n, stride, me, index - me * stride))
    for n, stride, me, base in infos:

        def greet(k, carry, n=n, stride=stride, me=me, base=base):
            j = lax.rem(me + k, n)
            pl.semaphore_signal(
                barrier, inc=1, device_id=peer(axis, base + j * stride), device_id_type=MESH
            )
            return carry

        lax.fori_loop(1, n, greet, 0)
    pl.semaphore_wait(barrier, sum(n - 1 for n, _ in groups))

    def remote(g, k, direction):
        n, stride, me, base = infos[g]
        other = lax.rem(me + direction * k + n, n)
        return pltpu.make_async_remote_copy(
            src_ref=x_refs[g].at[other],
            dst_ref=y_refs[g].at[k - 1],
            send_sem=sems[2 * g].at[k - 1],
            recv_sem=sems[2 * g + 1].at[k - 1],
            device_id=peer(axis, base + other * stride),
            device_id_type=MESH,
        )

    for g in range(m):

        def send(k, carry, g=g):
            remote(g, k, 1).start()
            return carry

        lax.fori_loop(1, groups[g][0], send, 0)
    for g in range(m):

        def finish(k, carry, g=g):
            remote(g, k, 1).wait_send()
            remote(g, k, -1).wait_recv()
            return carry

        lax.fori_loop(1, groups[g][0], finish, 0)


def multi_sum(xs, axis, groups, cid):
    sems = []
    for n, _ in groups:
        sems += [pltpu.SemaphoreType.DMA((n - 1,)), pltpu.SemaphoreType.DMA((n - 1,))]
    ys = pl.pallas_call(
        functools.partial(multi_sum_kernel, axis, tuple(groups)),
        out_shape=[
            jax.ShapeDtypeStruct((n - 1,) + x.shape[1:], x.dtype) for x, (n, _) in zip(xs, groups)
        ],
        in_specs=[pl.BlockSpec(memory_space=pl.ANY)] * len(xs),
        out_specs=[pl.BlockSpec(memory_space=pl.ANY)] * len(xs),
        scratch_shapes=sems,
        compiler_params=pltpu.CompilerParams(collective_id=cid, has_side_effects=True),
    )(*xs)
    out = []
    for x, y, (n, stride) in zip(xs, ys, groups):
        own = lax.dynamic_index_in_dim(x, digit(axis, n, stride), 0, keepdims=False)
        out.append(own + jnp.sum(y, axis=0))
    return out


def seq_sum_scatter_2d(x, digits, ids):
    if len(digits) != 2:
        return lax.psum_scatter(x, "seq", scatter_dimension=0, tiled=True)
    (ns, ss), (nf, sf) = digits
    half = x.shape[1] // 2
    width = x.shape[1] - half
    a = reorder_blocks(x[:, :half], [ns, nf]).reshape((nf, -1, half))
    b = x[:, half:].reshape((ns, -1, width))
    a, b = multi_sum([a, b], "seq", [(nf, sf), (ns, ss)], ids.take())
    a = a.reshape((ns, -1, half))
    b = b.reshape((nf, -1, width))
    a, b = multi_sum([a, b], "seq", [(ns, ss), (nf, sf)], ids.take())
    return jnp.concatenate([a, b], axis=1)


class Ids:
    def __init__(self):
        self.next = 0

    def take(self):
        self.next += 1
        return self.next - 1


def exchange(x, axis, n, stride, gather, cid, absolute=False):
    slots = n if absolute and gather else n - 1
    shape = (slots,) + (x.shape if gather else x.shape[1:])
    return pl.pallas_call(
        functools.partial(exchange_kernel, axis, n, stride, gather, absolute),
        out_shape=jax.ShapeDtypeStruct(shape, x.dtype),
        in_specs=[pl.BlockSpec(memory_space=pl.ANY)],
        out_specs=pl.BlockSpec(memory_space=pl.ANY),
        scratch_shapes=[
            pltpu.SemaphoreType.DMA((n - 1,)),
            pltpu.SemaphoreType.DMA((slots,)),
        ],
        compiler_params=pltpu.CompilerParams(collective_id=cid, has_side_effects=True),
    )(x)


def gather_rows(x, axis, digits, ids):
    for n, stride in digits:
        x = jnp.concatenate([x[None], exchange(x, axis, n, stride, True, ids.take())])
    return x.reshape((-1,) + x.shape[-1:])


def sum_scatter_rows(x, axis, digits, ids):
    for n, stride in reversed(digits):
        x = x.reshape((n, -1) + x.shape[-1:])
        x = x[0] + jnp.sum(exchange(x, axis, n, stride, False, ids.take()), axis=0)
    return x


def digit(axis, n, stride):
    return lax.rem(lax.axis_index(axis) // stride, n)


def gather_rows_absolute(x, axis, digits, ids):
    for n, stride in digits:
        y = exchange(x, axis, n, stride, True, ids.take(), absolute=True)
        x = lax.dynamic_update_index_in_dim(y, x, digit(axis, n, stride), 0)
    return x.reshape((-1,) + x.shape[-1:])


def sum_scatter_rows_absolute(x, axis, digits, ids):
    for n, stride in reversed(digits):
        x = x.reshape((n, -1) + x.shape[-1:])
        own = lax.dynamic_index_in_dim(x, digit(axis, n, stride), 0, keepdims=False)
        x = own + jnp.sum(exchange(x, axis, n, stride, False, ids.take(), absolute=True), axis=0)
    return x


def reorder_blocks(x, sizes):
    k = len(sizes)
    x = x.reshape(tuple(sizes) + (-1, x.shape[-1]))
    x = jnp.transpose(x, tuple(reversed(range(k))) + (k, k + 1))
    return x.reshape((-1, x.shape[-1]))


def seq_sum_scatter(x, digits, ids):
    x = reorder_blocks(x, [n for n, _ in digits])
    return sum_scatter_rows_absolute(x, "seq", digits, ids)


def seq_gather(x, digits, ids):
    x = gather_rows_absolute(x, "seq", digits, ids)
    return reorder_blocks(x, [n for n, _ in reversed(digits)])


def widen(mask, rows):
    block = rows // mask.shape[0]
    full = jnp.repeat(jnp.repeat(mask, block, axis=0), block, axis=1)
    return full.astype(jnp.bfloat16)


def gating(summed, width):
    gate = summed[:, :width]
    up = summed[:, width:]
    sig = jax.nn.sigmoid(gate)
    act = gate * sig
    return (gate, up, sig, act)


def gate_up_grads(gate, up, sig, act, grad_hidden):
    dgate = (grad_hidden * up * sig * (1.0 + gate * (1.0 - sig))).astype(jnp.bfloat16)
    dup = (grad_hidden * act).astype(jnp.bfloat16)
    return jnp.concatenate([dgate, dup], axis=1)


def per_device(tensor_digits, seq_digits, tokens, w_gate, w_up, w_down, mask_gate, mask_up, mask_down, cotangent):
    width = w_gate.shape[1]
    feat = tokens.shape[1]
    gate_mask = widen(mask_gate, w_gate.shape[0])
    up_mask = widen(mask_up, w_up.shape[0])
    down_mask = widen(mask_down, w_down.shape[0])
    joined = jnp.concatenate([w_gate * gate_mask, w_up * up_mask], axis=1)
    down_w = w_down * down_mask
    contract_first = (((0,), (0,)), ((), ()))
    contract_last = (((1,), (1,)), ((), ()))
    ids = Ids()
    both = gather_rows(jnp.concatenate([tokens, cotangent], axis=1), "tensor", tensor_digits, ids)
    gathered = both[:, :feat]
    cot_rows = both[:, feat:]
    partial_value = jnp.dot(gathered, joined, preferred_element_type=jnp.float32)
    summed = seq_sum_scatter_2d(partial_value, seq_digits, ids)
    gate, up, sig, act = gating(summed, width)
    hidden_part = (act * up).astype(jnp.bfloat16)
    hidden = seq_gather(hidden_part, seq_digits, ids)
    output = sum_scatter_rows(
        jnp.dot(hidden, down_w, preferred_element_type=jnp.float32), "tensor", tensor_digits, ids
    ).astype(jnp.bfloat16)
    grad_part = lax.dot_general(cot_rows, down_w, contract_last, preferred_element_type=jnp.float32)
    grad_hidden = seq_sum_scatter_2d(grad_part, seq_digits, ids)
    grads_part = gate_up_grads(gate, up, sig, act, grad_hidden)
    grads_part, hidden = lax.optimization_barrier((grads_part, hidden))
    grads = lax.all_gather(grads_part, "seq", axis=0, tiled=True)
    grad_tokens = sum_scatter_rows(
        lax.dot_general(grads, joined, contract_last, preferred_element_type=jnp.float32),
        "tensor",
        tensor_digits,
        ids,
    ).astype(jnp.bfloat16)
    weight_grad = lax.dot_general(
        gathered, grads, contract_first, preferred_element_type=jnp.float32
    )
    grad_gate = (weight_grad[:, :width] * gate_mask).astype(jnp.bfloat16)
    grad_up = (weight_grad[:, width:] * up_mask).astype(jnp.bfloat16)
    down_grad = lax.dot_general(
        hidden, cot_rows, contract_first, preferred_element_type=jnp.float32
    )
    grad_down = (down_grad * down_mask).astype(jnp.bfloat16)
    return (output, grad_tokens, grad_gate, grad_up, grad_down)


def axis_parts(mesh, axis):
    n = mesh.shape[axis]
    line = np.moveaxis(mesh.devices, mesh.axis_names.index(axis), -1).reshape(-1, n)[0]
    try:
        keys = [tuple(d.coords) + (d.core_on_chip,) for d in line]
    except AttributeError:
        return [n]
    parts, stride = [], 1
    while stride < n:
        changed = [c for c in range(len(keys[0])) if keys[stride][c] != keys[0][c]]
        size = 1
        while stride * size < n:
            moved = [c for c in range(len(keys[0])) if keys[stride * size][c] != keys[0][c]]
            if moved != changed:
                break
            size += 1
        if (n // stride) % size:
            return [n]
        parts.append(size)
        stride *= size
    return parts[::-1]


def digits_of(mesh, axis):
    sizes = axis_parts(mesh, axis)
    digits, stride = [], 1
    for n in reversed(sizes):
        if n > 1:
            digits.append((n, stride))
        stride *= n
    return tuple(reversed(digits))


def solution(mesh):
    return jax.shard_map(
        functools.partial(per_device, digits_of(mesh, "tensor"), digits_of(mesh, "seq")),
        mesh=mesh,
        in_specs=(
            P("tensor", "seq"),
            P("seq", "tensor"),
            P("seq", "tensor"),
            P("tensor", "seq"),
            P("seq", "tensor"),
            P("seq", "tensor"),
            P("tensor", "seq"),
            P("tensor", "seq"),
        ),
        out_specs=(
            P("tensor", "seq"),
            P("tensor", "seq"),
            P("seq", "tensor"),
            P("seq", "tensor"),
            P("tensor", "seq"),
        ),
        check_vma=False,
    )
```

```python
import functools

import jax
import numpy as np
import jax.numpy as jnp
from jax import lax
from jax.experimental import pallas as pl
from jax.experimental.pallas import tpu as pltpu
from jax.sharding import PartitionSpec as P

MESH = pl.DeviceIdType.MESH
AXES = ("seq", "tensor")


def peer(axis, j):
    return tuple(j if a == axis else lax.axis_index(a) for a in AXES)


def exchange_kernel(axis, n, stride, gather, absolute, x_ref, y_ref, send_sem, recv_sem):
    index = lax.axis_index(axis)
    me = lax.rem(index // stride, n)
    base = index - me * stride
    barrier = pltpu.get_barrier_semaphore()

    def device(j):
        return peer(axis, base + j * stride)

    def greet(k, carry):
        pl.semaphore_signal(
            barrier, inc=1, device_id=device(lax.rem(me + k, n)), device_id_type=MESH
        )
        return carry

    lax.fori_loop(1, n, greet, 0)
    pl.semaphore_wait(barrier, n - 1)

    def remote(k, direction):
        other = lax.rem(me + direction * k + n, n)
        if absolute and gather:
            slot = me if direction == ahead else other
        else:
            slot = k - 1
        return pltpu.make_async_remote_copy(
            src_ref=x_ref if gather else x_ref.at[other if absolute else k],
            dst_ref=y_ref.at[slot],
            send_sem=send_sem.at[k - 1],
            recv_sem=recv_sem.at[slot],
            device_id=device(other),
            device_id_type=MESH,
        )

    ahead = 1 if absolute or not gather else -1

    def send(k, carry):
        remote(k, ahead).start()
        return carry

    lax.fori_loop(1, n, send, 0)

    def finish(k, carry):
        remote(k, ahead).wait_send()
        remote(k, -ahead).wait_recv()
        return carry

    lax.fori_loop(1, n, finish, 0)


def multi_sum_kernel(axis, groups, *refs):
    m = len(groups)
    x_refs, y_refs, sems = refs[:m], refs[m:2 * m], refs[2 * m:]
    index = lax.axis_index(axis)
    barrier = pltpu.get_barrier_semaphore()
    infos = []
    for n, stride in groups:
        me = lax.rem(index // stride, n)
        infos.append((n, stride, me, index - me * stride))
    for n, stride, me, base in infos:

        def greet(k, carry, n=n, stride=stride, me=me, base=base):
            j = lax.rem(me + k, n)
            pl.semaphore_signal(
                barrier, inc=1, device_id=peer(axis, base + j * stride), device_id_type=MESH
            )
            return carry

        lax.fori_loop(1, n, greet, 0)
    pl.semaphore_wait(barrier, sum(n - 1 for n, _ in groups))

    def remote(g, k, direction):
        n, stride, me, base = infos[g]
        other = lax.rem(me + direction * k + n, n)
        return pltpu.make_async_remote_copy(
            src_ref=x_refs[g].at[other],
            dst_ref=y_refs[g].at[k - 1],
            send_sem=sems[2 * g].at[k - 1],
            recv_sem=sems[2 * g + 1].at[k - 1],
            device_id=peer(axis, base + other * stride),
            device_id_type=MESH,
        )

    for g in range(m):

        def send(k, carry, g=g):
            remote(g, k, 1).start()
            return carry

        lax.fori_loop(1, groups[g][0], send, 0)
    for g in range(m):

        def finish(k, carry, g=g):
            remote(g, k, 1).wait_send()
            remote(g, k, -1).wait_recv()
            return carry

        lax.fori_loop(1, groups[g][0], finish, 0)


def multi_sum(xs, axis, groups, cid):
    sems = []
    for n, _ in groups:
        sems += [pltpu.SemaphoreType.DMA((n - 1,)), pltpu.SemaphoreType.DMA((n - 1,))]
    ys = pl.pallas_call(
        functools.partial(multi_sum_kernel, axis, tuple(groups)),
        out_shape=[
            jax.ShapeDtypeStruct((n - 1,) + x.shape[1:], x.dtype) for x, (n, _) in zip(xs, groups)
        ],
        in_specs=[pl.BlockSpec(memory_space=pl.ANY)] * len(xs),
        out_specs=[pl.BlockSpec(memory_space=pl.ANY)] * len(xs),
        scratch_shapes=sems,
        compiler_params=pltpu.CompilerParams(collective_id=cid, has_side_effects=True),
    )(*xs)
    out = []
    for x, y, (n, stride) in zip(xs, ys, groups):
        own = lax.dynamic_index_in_dim(x, digit(axis, n, stride), 0, keepdims=False)
        out.append(own + jnp.sum(y, axis=0))
    return out


def seq_sum_scatter_2d(x, digits, ids):
    if len(digits) != 2:
        return lax.psum_scatter(x, "seq", scatter_dimension=0, tiled=True)
    (ns, ss), (nf, sf) = digits
    half = x.shape[1] // 2
    width = x.shape[1] - half
    a = reorder_blocks(x[:, :half], [ns, nf]).reshape((nf, -1, half))
    b = x[:, half:].reshape((ns, -1, width))
    a, b = multi_sum([a, b], "seq", [(nf, sf), (ns, ss)], ids.take())
    a = a.reshape((ns, -1, half))
    b = b.reshape((nf, -1, width))
    a, b = multi_sum([a, b], "seq", [(ns, ss), (nf, sf)], ids.take())
    return jnp.concatenate([a, b], axis=1)


class Ids:
    def __init__(self):
        self.next = 0

    def take(self):
        self.next += 1
        return self.next - 1


def exchange(x, axis, n, stride, gather, cid, absolute=False):
    slots = n if absolute and gather else n - 1
    shape = (slots,) + (x.shape if gather else x.shape[1:])
    return pl.pallas_call(
        functools.partial(exchange_kernel, axis, n, stride, gather, absolute),
        out_shape=jax.ShapeDtypeStruct(shape, x.dtype),
        in_specs=[pl.BlockSpec(memory_space=pl.ANY)],
        out_specs=pl.BlockSpec(memory_space=pl.ANY),
        scratch_shapes=[
            pltpu.SemaphoreType.DMA((n - 1,)),
            pltpu.SemaphoreType.DMA((slots,)),
        ],
        compiler_params=pltpu.CompilerParams(collective_id=cid, has_side_effects=True),
    )(x)


def gather_rows(x, axis, digits, ids):
    for n, stride in digits:
        x = jnp.concatenate([x[None], exchange(x, axis, n, stride, True, ids.take())])
    return x.reshape((-1,) + x.shape[-1:])


def sum_scatter_rows(x, axis, digits, ids):
    for n, stride in reversed(digits):
        x = x.reshape((n, -1) + x.shape[-1:])
        x = x[0] + jnp.sum(exchange(x, axis, n, stride, False, ids.take()), axis=0)
    return x


def digit(axis, n, stride):
    return lax.rem(lax.axis_index(axis) // stride, n)


def gather_rows_absolute(x, axis, digits, ids):
    for n, stride in digits:
        y = exchange(x, axis, n, stride, True, ids.take(), absolute=True)
        x = lax.dynamic_update_index_in_dim(y, x, digit(axis, n, stride), 0)
    return x.reshape((-1,) + x.shape[-1:])


def sum_scatter_rows_absolute(x, axis, digits, ids):
    for n, stride in reversed(digits):
        x = x.reshape((n, -1) + x.shape[-1:])
        own = lax.dynamic_index_in_dim(x, digit(axis, n, stride), 0, keepdims=False)
        x = own + jnp.sum(exchange(x, axis, n, stride, False, ids.take(), absolute=True), axis=0)
    return x


def reorder_blocks(x, sizes):
    k = len(sizes)
    x = x.reshape(tuple(sizes) + (-1, x.shape[-1]))
    x = jnp.transpose(x, tuple(reversed(range(k))) + (k, k + 1))
    return x.reshape((-1, x.shape[-1]))


def seq_sum_scatter(x, digits, ids):
    x = reorder_blocks(x, [n for n, _ in digits])
    return sum_scatter_rows_absolute(x, "seq", digits, ids)


def seq_gather(x, digits, ids):
    x = gather_rows_absolute(x, "seq", digits, ids)
    return reorder_blocks(x, [n for n, _ in reversed(digits)])


def widen(mask, rows):
    block = rows // mask.shape[0]
    full = jnp.repeat(jnp.repeat(mask, block, axis=0), block, axis=1)
    return full.astype(jnp.bfloat16)


def gating(summed, width):
    gate = summed[:, :width]
    up = summed[:, width:]
    sig = jax.nn.sigmoid(gate)
    act = gate * sig
    return (gate, up, sig, act)


def gate_up_grads(gate, up, sig, act, grad_hidden):
    dgate = (grad_hidden * up * sig * (1.0 + gate * (1.0 - sig))).astype(jnp.bfloat16)
    dup = (grad_hidden * act).astype(jnp.bfloat16)
    return jnp.concatenate([dgate, dup], axis=1)


def per_device(tensor_digits, seq_digits, tokens, w_gate, w_up, w_down, mask_gate, mask_up, mask_down, cotangent):
    width = w_gate.shape[1]
    feat = tokens.shape[1]
    gate_mask = widen(mask_gate, w_gate.shape[0])
    up_mask = widen(mask_up, w_up.shape[0])
    down_mask = widen(mask_down, w_down.shape[0])
    joined = jnp.concatenate([w_gate * gate_mask, w_up * up_mask], axis=1)
    down_w = w_down * down_mask
    contract_first = (((0,), (0,)), ((), ()))
    contract_last = (((1,), (1,)), ((), ()))
    ids = Ids()
    cot_rows = gather_rows(cotangent, "tensor", tensor_digits, ids)
    grad_part = lax.dot_general(cot_rows, down_w, contract_last, preferred_element_type=jnp.float32)
    grad_part, tokens = lax.optimization_barrier((grad_part, tokens))
    grad_hidden = lax.psum_scatter(grad_part, "seq", scatter_dimension=0, tiled=True)
    gathered = gather_rows(tokens, "tensor", tensor_digits, ids)
    partial_value = jnp.dot(gathered, joined, preferred_element_type=jnp.float32)
    summed = seq_sum_scatter_2d(partial_value, seq_digits, ids)
    gate, up, sig, act = gating(summed, width)
    hidden_part = (act * up).astype(jnp.bfloat16)
    hidden = seq_gather(hidden_part, seq_digits, ids)
    output = sum_scatter_rows(
        jnp.dot(hidden, down_w, preferred_element_type=jnp.float32), "tensor", tensor_digits, ids
    ).astype(jnp.bfloat16)
    grads_part = gate_up_grads(gate, up, sig, act, grad_hidden)
    grads_part, hidden = lax.optimization_barrier((grads_part, hidden))
    grads = lax.all_gather(grads_part, "seq", axis=0, tiled=True)
    grad_tokens = sum_scatter_rows(
        lax.dot_general(grads, joined, contract_last, preferred_element_type=jnp.float32),
        "tensor",
        tensor_digits,
        ids,
    ).astype(jnp.bfloat16)
    weight_grad = lax.dot_general(
        gathered, grads, contract_first, preferred_element_type=jnp.float32
    )
    grad_gate = (weight_grad[:, :width] * gate_mask).astype(jnp.bfloat16)
    grad_up = (weight_grad[:, width:] * up_mask).astype(jnp.bfloat16)
    down_grad = lax.dot_general(
        hidden, cot_rows, contract_first, preferred_element_type=jnp.float32
    )
    grad_down = (down_grad * down_mask).astype(jnp.bfloat16)
    return (output, grad_tokens, grad_gate, grad_up, grad_down)


def axis_parts(mesh, axis):
    n = mesh.shape[axis]
    line = np.moveaxis(mesh.devices, mesh.axis_names.index(axis), -1).reshape(-1, n)[0]
    try:
        keys = [tuple(d.coords) + (d.core_on_chip,) for d in line]
    except AttributeError:
        return [n]
    parts, stride = [], 1
    while stride < n:
        changed = [c for c in range(len(keys[0])) if keys[stride][c] != keys[0][c]]
        size = 1
        while stride * size < n:
            moved = [c for c in range(len(keys[0])) if keys[stride * size][c] != keys[0][c]]
            if moved != changed:
                break
            size += 1
        if (n // stride) % size:
            return [n]
        parts.append(size)
        stride *= size
    return parts[::-1]


def digits_of(mesh, axis):
    sizes = axis_parts(mesh, axis)
    digits, stride = [], 1
    for n in reversed(sizes):
        if n > 1:
            digits.append((n, stride))
        stride *= n
    return tuple(reversed(digits))


def solution(mesh):
    return jax.shard_map(
        functools.partial(per_device, digits_of(mesh, "tensor"), digits_of(mesh, "seq")),
        mesh=mesh,
        in_specs=(
            P("tensor", "seq"),
            P("seq", "tensor"),
            P("seq", "tensor"),
            P("tensor", "seq"),
            P("seq", "tensor"),
            P("seq", "tensor"),
            P("tensor", "seq"),
            P("tensor", "seq"),
        ),
        out_specs=(
            P("tensor", "seq"),
            P("tensor", "seq"),
            P("seq", "tensor"),
            P("seq", "tensor"),
            P("tensor", "seq"),
        ),
        check_vma=False,
    )
```

```python
import functools

import jax
import numpy as np
import jax.numpy as jnp
from jax import lax
from jax.experimental import pallas as pl
from jax.experimental.pallas import tpu as pltpu
from jax.sharding import PartitionSpec as P

MESH = pl.DeviceIdType.MESH
AXES = ("seq", "tensor")


def peer(axis, j):
    return tuple(j if a == axis else lax.axis_index(a) for a in AXES)


def exchange_kernel(axis, n, stride, gather, absolute, x_ref, y_ref, send_sem, recv_sem):
    index = lax.axis_index(axis)
    me = lax.rem(index // stride, n)
    base = index - me * stride
    barrier = pltpu.get_barrier_semaphore()

    def device(j):
        return peer(axis, base + j * stride)

    def greet(k, carry):
        pl.semaphore_signal(
            barrier, inc=1, device_id=device(lax.rem(me + k, n)), device_id_type=MESH
        )
        return carry

    lax.fori_loop(1, n, greet, 0)
    pl.semaphore_wait(barrier, n - 1)

    def remote(k, direction):
        other = lax.rem(me + direction * k + n, n)
        if absolute and gather:
            slot = me if direction == ahead else other
        else:
            slot = k - 1
        return pltpu.make_async_remote_copy(
            src_ref=x_ref if gather else x_ref.at[other if absolute else k],
            dst_ref=y_ref.at[slot],
            send_sem=send_sem.at[k - 1],
            recv_sem=recv_sem.at[slot],
            device_id=device(other),
            device_id_type=MESH,
        )

    ahead = 1 if absolute or not gather else -1

    def send(k, carry):
        remote(k, ahead).start()
        return carry

    lax.fori_loop(1, n, send, 0)

    def finish(k, carry):
        remote(k, ahead).wait_send()
        remote(k, -ahead).wait_recv()
        return carry

    lax.fori_loop(1, n, finish, 0)


def multi_sum_kernel(axis, groups, relative, *refs):
    m = len(groups)
    x_refs, y_refs, sems = refs[:m], refs[m:2 * m], refs[2 * m:]
    index = lax.axis_index(axis)
    barrier = pltpu.get_barrier_semaphore()
    infos = []
    for n, stride in groups:
        me = lax.rem(index // stride, n)
        infos.append((n, stride, me, index - me * stride))
    for n, stride, me, base in infos:

        def greet(k, carry, n=n, stride=stride, me=me, base=base):
            j = lax.rem(me + k, n)
            pl.semaphore_signal(
                barrier, inc=1, device_id=peer(axis, base + j * stride), device_id_type=MESH
            )
            return carry

        lax.fori_loop(1, n, greet, 0)
    pl.semaphore_wait(barrier, sum(n - 1 for n, _ in groups))

    def remote(g, k, direction):
        n, stride, me, base = infos[g]
        other = lax.rem(me + direction * k + n, n)
        return pltpu.make_async_remote_copy(
            src_ref=x_refs[g].at[k if relative else other],
            dst_ref=y_refs[g].at[k - 1],
            send_sem=sems[2 * g].at[k - 1],
            recv_sem=sems[2 * g + 1].at[k - 1],
            device_id=peer(axis, base + other * stride),
            device_id_type=MESH,
        )

    for g in range(m):

        def send(k, carry, g=g):
            remote(g, k, 1).start()
            return carry

        lax.fori_loop(1, groups[g][0], send, 0)
    for g in range(m):

        def finish(k, carry, g=g):
            remote(g, k, 1).wait_send()
            remote(g, k, -1).wait_recv()
            return carry

        lax.fori_loop(1, groups[g][0], finish, 0)


def multi_sum(xs, axis, groups, cid, relative=False):
    sems = []
    for n, _ in groups:
        sems += [pltpu.SemaphoreType.DMA((n - 1,)), pltpu.SemaphoreType.DMA((n - 1,))]
    ys = pl.pallas_call(
        functools.partial(multi_sum_kernel, axis, tuple(groups), relative),
        out_shape=[
            jax.ShapeDtypeStruct((n - 1,) + x.shape[1:], x.dtype) for x, (n, _) in zip(xs, groups)
        ],
        in_specs=[pl.BlockSpec(memory_space=pl.ANY)] * len(xs),
        out_specs=[pl.BlockSpec(memory_space=pl.ANY)] * len(xs),
        scratch_shapes=sems,
        compiler_params=pltpu.CompilerParams(collective_id=cid, has_side_effects=True),
    )(*xs)
    out = []
    for x, y, (n, stride) in zip(xs, ys, groups):
        if relative:
            own = x[0]
        else:
            own = lax.dynamic_index_in_dim(x, digit(axis, n, stride), 0, keepdims=False)
        out.append(own + jnp.sum(y, axis=0))
    return out


def tensor_sum_scatter(x, digits, ids):
    if len(digits) != 3:
        return sum_scatter_rows(x, "tensor", digits, ids)
    (nf, sf), (nn, sn), (nc, sc) = digits
    cols = x.shape[-1]
    x = x.reshape((nc, -1, cols))
    x = x[0] + jnp.sum(exchange(x, "tensor", nc, sc, False, ids.take()), axis=0)
    half = cols // 2
    a = x[:, :half].reshape((nn, -1, half))
    b = x[:, half:].reshape((nn, nf, -1, cols - half))
    b = jnp.swapaxes(b, 0, 1).reshape((nf, -1, cols - half))
    a, b = multi_sum([a, b], "tensor", [(nn, sn), (nf, sf)], ids.take(), relative=True)
    a = a.reshape((nf, -1, half))
    b = b.reshape((nn, -1, cols - half))
    a, b = multi_sum([a, b], "tensor", [(nf, sf), (nn, sn)], ids.take(), relative=True)
    return jnp.concatenate([a, b], axis=1)


def seq_sum_scatter_2d(x, digits, ids):
    if len(digits) != 2:
        return lax.psum_scatter(x, "seq", scatter_dimension=0, tiled=True)
    (ns, ss), (nf, sf) = digits
    half = x.shape[1] // 2
    width = x.shape[1] - half
    a = reorder_blocks(x[:, :half], [ns, nf]).reshape((nf, -1, half))
    b = x[:, half:].reshape((ns, -1, width))
    a, b = multi_sum([a, b], "seq", [(nf, sf), (ns, ss)], ids.take())
    a = a.reshape((ns, -1, half))
    b = b.reshape((nf, -1, width))
    a, b = multi_sum([a, b], "seq", [(ns, ss), (nf, sf)], ids.take())
    return jnp.concatenate([a, b], axis=1)


class Ids:
    def __init__(self):
        self.next = 0

    def take(self):
        self.next += 1
        return self.next - 1


def exchange(x, axis, n, stride, gather, cid, absolute=False):
    slots = n if absolute and gather else n - 1
    shape = (slots,) + (x.shape if gather else x.shape[1:])
    return pl.pallas_call(
        functools.partial(exchange_kernel, axis, n, stride, gather, absolute),
        out_shape=jax.ShapeDtypeStruct(shape, x.dtype),
        in_specs=[pl.BlockSpec(memory_space=pl.ANY)],
        out_specs=pl.BlockSpec(memory_space=pl.ANY),
        scratch_shapes=[
            pltpu.SemaphoreType.DMA((n - 1,)),
            pltpu.SemaphoreType.DMA((slots,)),
        ],
        compiler_params=pltpu.CompilerParams(collective_id=cid, has_side_effects=True),
    )(x)


def gather_rows(x, axis, digits, ids):
    for n, stride in digits:
        x = jnp.concatenate([x[None], exchange(x, axis, n, stride, True, ids.take())])
    return x.reshape((-1,) + x.shape[-1:])


def sum_scatter_rows(x, axis, digits, ids):
    for n, stride in reversed(digits):
        x = x.reshape((n, -1) + x.shape[-1:])
        x = x[0] + jnp.sum(exchange(x, axis, n, stride, False, ids.take()), axis=0)
    return x


def digit(axis, n, stride):
    return lax.rem(lax.axis_index(axis) // stride, n)


def gather_rows_absolute(x, axis, digits, ids):
    for n, stride in digits:
        y = exchange(x, axis, n, stride, True, ids.take(), absolute=True)
        x = lax.dynamic_update_index_in_dim(y, x, digit(axis, n, stride), 0)
    return x.reshape((-1,) + x.shape[-1:])


def sum_scatter_rows_absolute(x, axis, digits, ids):
    for n, stride in reversed(digits):
        x = x.reshape((n, -1) + x.shape[-1:])
        own = lax.dynamic_index_in_dim(x, digit(axis, n, stride), 0, keepdims=False)
        x = own + jnp.sum(exchange(x, axis, n, stride, False, ids.take(), absolute=True), axis=0)
    return x


def reorder_blocks(x, sizes):
    k = len(sizes)
    x = x.reshape(tuple(sizes) + (-1, x.shape[-1]))
    x = jnp.transpose(x, tuple(reversed(range(k))) + (k, k + 1))
    return x.reshape((-1, x.shape[-1]))


def seq_sum_scatter(x, digits, ids):
    x = reorder_blocks(x, [n for n, _ in digits])
    return sum_scatter_rows_absolute(x, "seq", digits, ids)


def seq_gather(x, digits, ids):
    x = gather_rows_absolute(x, "seq", digits, ids)
    return reorder_blocks(x, [n for n, _ in reversed(digits)])


def widen(mask, rows):
    block = rows // mask.shape[0]
    full = jnp.repeat(jnp.repeat(mask, block, axis=0), block, axis=1)
    return full.astype(jnp.bfloat16)


def gating(summed, width):
    gate = summed[:, :width]
    up = summed[:, width:]
    sig = jax.nn.sigmoid(gate)
    act = gate * sig
    return (gate, up, sig, act)


def gate_up_grads(gate, up, sig, act, grad_hidden):
    dgate = (grad_hidden * up * sig * (1.0 + gate * (1.0 - sig))).astype(jnp.bfloat16)
    dup = (grad_hidden * act).astype(jnp.bfloat16)
    return jnp.concatenate([dgate, dup], axis=1)


def per_device(tensor_digits, seq_digits, tokens, w_gate, w_up, w_down, mask_gate, mask_up, mask_down, cotangent):
    width = w_gate.shape[1]
    feat = tokens.shape[1]
    gate_mask = widen(mask_gate, w_gate.shape[0])
    up_mask = widen(mask_up, w_up.shape[0])
    down_mask = widen(mask_down, w_down.shape[0])
    joined = jnp.concatenate([w_gate * gate_mask, w_up * up_mask], axis=1)
    down_w = w_down * down_mask
    contract_first = (((0,), (0,)), ((), ()))
    contract_last = (((1,), (1,)), ((), ()))
    ids = Ids()
    cot_rows = gather_rows(cotangent, "tensor", tensor_digits, ids)
    grad_part = lax.dot_general(cot_rows, down_w, contract_last, preferred_element_type=jnp.float32)
    grad_part, tokens = lax.optimization_barrier((grad_part, tokens))
    grad_hidden = lax.psum_scatter(grad_part, "seq", scatter_dimension=0, tiled=True)
    gathered = gather_rows(tokens, "tensor", tensor_digits, ids)
    partial_value = jnp.dot(gathered, joined, preferred_element_type=jnp.float32)
    summed = seq_sum_scatter_2d(partial_value, seq_digits, ids)
    gate, up, sig, act = gating(summed, width)
    hidden_part = (act * up).astype(jnp.bfloat16)
    hidden = seq_gather(hidden_part, seq_digits, ids)
    output = tensor_sum_scatter(
        jnp.dot(hidden, down_w, preferred_element_type=jnp.float32), tensor_digits, ids
    ).astype(jnp.bfloat16)
    grads_part = gate_up_grads(gate, up, sig, act, grad_hidden)
    grads_part, hidden = lax.optimization_barrier((grads_part, hidden))
    grads = lax.all_gather(grads_part, "seq", axis=0, tiled=True)
    grad_tokens = tensor_sum_scatter(
        lax.dot_general(grads, joined, contract_last, preferred_element_type=jnp.float32),
        tensor_digits,
        ids,
    ).astype(jnp.bfloat16)
    weight_grad = lax.dot_general(
        gathered, grads, contract_first, preferred_element_type=jnp.float32
    )
    grad_gate = (weight_grad[:, :width] * gate_mask).astype(jnp.bfloat16)
    grad_up = (weight_grad[:, width:] * up_mask).astype(jnp.bfloat16)
    down_grad = lax.dot_general(
        hidden, cot_rows, contract_first, preferred_element_type=jnp.float32
    )
    grad_down = (down_grad * down_mask).astype(jnp.bfloat16)
    return (output, grad_tokens, grad_gate, grad_up, grad_down)


def axis_parts(mesh, axis):
    n = mesh.shape[axis]
    line = np.moveaxis(mesh.devices, mesh.axis_names.index(axis), -1).reshape(-1, n)[0]
    try:
        keys = [tuple(d.coords) + (d.core_on_chip,) for d in line]
    except AttributeError:
        return [n]
    parts, stride = [], 1
    while stride < n:
        changed = [c for c in range(len(keys[0])) if keys[stride][c] != keys[0][c]]
        size = 1
        while stride * size < n:
            moved = [c for c in range(len(keys[0])) if keys[stride * size][c] != keys[0][c]]
            if moved != changed:
                break
            size += 1
        if (n // stride) % size:
            return [n]
        parts.append(size)
        stride *= size
    return parts[::-1]


def digits_of(mesh, axis):
    sizes = axis_parts(mesh, axis)
    digits, stride = [], 1
    for n in reversed(sizes):
        if n > 1:
            digits.append((n, stride))
        stride *= n
    return tuple(reversed(digits))


def solution(mesh):
    return jax.shard_map(
        functools.partial(per_device, digits_of(mesh, "tensor"), digits_of(mesh, "seq")),
        mesh=mesh,
        in_specs=(
            P("tensor", "seq"),
            P("seq", "tensor"),
            P("seq", "tensor"),
            P("tensor", "seq"),
            P("seq", "tensor"),
            P("seq", "tensor"),
            P("tensor", "seq"),
            P("tensor", "seq"),
        ),
        out_specs=(
            P("tensor", "seq"),
            P("tensor", "seq"),
            P("seq", "tensor"),
            P("seq", "tensor"),
            P("tensor", "seq"),
        ),
        check_vma=False,
    )
```

```python
import functools

import jax
import numpy as np
import jax.numpy as jnp
from jax import lax
from jax.experimental import pallas as pl
from jax.experimental.pallas import tpu as pltpu
from jax.sharding import PartitionSpec as P

MESH = pl.DeviceIdType.MESH
AXES = ("seq", "tensor")


def peer(axis, j):
    return tuple(j if a == axis else lax.axis_index(a) for a in AXES)


def exchange_kernel(axis, n, stride, gather, absolute, x_ref, y_ref, send_sem, recv_sem):
    index = lax.axis_index(axis)
    me = lax.rem(index // stride, n)
    base = index - me * stride
    barrier = pltpu.get_barrier_semaphore()

    def device(j):
        return peer(axis, base + j * stride)

    def greet(k, carry):
        pl.semaphore_signal(
            barrier, inc=1, device_id=device(lax.rem(me + k, n)), device_id_type=MESH
        )
        return carry

    lax.fori_loop(1, n, greet, 0)
    pl.semaphore_wait(barrier, n - 1)

    def remote(k, direction):
        other = lax.rem(me + direction * k + n, n)
        if absolute and gather:
            slot = me if direction == ahead else other
        else:
            slot = k - 1
        return pltpu.make_async_remote_copy(
            src_ref=x_ref if gather else x_ref.at[other if absolute else k],
            dst_ref=y_ref.at[slot],
            send_sem=send_sem.at[k - 1],
            recv_sem=recv_sem.at[slot],
            device_id=device(other),
            device_id_type=MESH,
        )

    ahead = 1 if absolute or not gather else -1

    def send(k, carry):
        remote(k, ahead).start()
        return carry

    lax.fori_loop(1, n, send, 0)

    def finish(k, carry):
        remote(k, ahead).wait_send()
        remote(k, -ahead).wait_recv()
        return carry

    lax.fori_loop(1, n, finish, 0)


def multi_sum_kernel(axis, groups, *refs):
    m = len(groups)
    x_refs, y_refs, sems = refs[:m], refs[m:2 * m], refs[2 * m:]
    index = lax.axis_index(axis)
    barrier = pltpu.get_barrier_semaphore()
    infos = []
    for n, stride in groups:
        me = lax.rem(index // stride, n)
        infos.append((n, stride, me, index - me * stride))
    for n, stride, me, base in infos:

        def greet(k, carry, n=n, stride=stride, me=me, base=base):
            j = lax.rem(me + k, n)
            pl.semaphore_signal(
                barrier, inc=1, device_id=peer(axis, base + j * stride), device_id_type=MESH
            )
            return carry

        lax.fori_loop(1, n, greet, 0)
    pl.semaphore_wait(barrier, sum(n - 1 for n, _ in groups))

    def remote(g, k, direction):
        n, stride, me, base = infos[g]
        other = lax.rem(me + direction * k + n, n)
        return pltpu.make_async_remote_copy(
            src_ref=x_refs[g].at[other],
            dst_ref=y_refs[g].at[k - 1],
            send_sem=sems[2 * g].at[k - 1],
            recv_sem=sems[2 * g + 1].at[k - 1],
            device_id=peer(axis, base + other * stride),
            device_id_type=MESH,
        )

    for g in range(m):

        def send(k, carry, g=g):
            remote(g, k, 1).start()
            return carry

        lax.fori_loop(1, groups[g][0], send, 0)
    for g in range(m):

        def finish(k, carry, g=g):
            remote(g, k, 1).wait_send()
            remote(g, k, -1).wait_recv()
            return carry

        lax.fori_loop(1, groups[g][0], finish, 0)


def multi_sum(xs, axis, groups, cid):
    sems = []
    for n, _ in groups:
        sems += [pltpu.SemaphoreType.DMA((n - 1,)), pltpu.SemaphoreType.DMA((n - 1,))]
    ys = pl.pallas_call(
        functools.partial(multi_sum_kernel, axis, tuple(groups)),
        out_shape=[
            jax.ShapeDtypeStruct((n - 1,) + x.shape[1:], x.dtype) for x, (n, _) in zip(xs, groups)
        ],
        in_specs=[pl.BlockSpec(memory_space=pl.ANY)] * len(xs),
        out_specs=[pl.BlockSpec(memory_space=pl.ANY)] * len(xs),
        scratch_shapes=sems,
        compiler_params=pltpu.CompilerParams(collective_id=cid, has_side_effects=True),
    )(*xs)
    out = []
    for x, y, (n, stride) in zip(xs, ys, groups):
        own = lax.dynamic_index_in_dim(x, digit(axis, n, stride), 0, keepdims=False)
        out.append(own + jnp.sum(y, axis=0))
    return out


def seq_sum_scatter_2d(x, digits, ids):
    if len(digits) != 2:
        return lax.psum_scatter(x, "seq", scatter_dimension=0, tiled=True)
    (ns, ss), (nf, sf) = digits
    half = x.shape[1] // 2
    width = x.shape[1] - half
    a = reorder_blocks(x[:, :half], [ns, nf]).reshape((nf, -1, half))
    b = x[:, half:].reshape((ns, -1, width))
    a, b = multi_sum([a, b], "seq", [(nf, sf), (ns, ss)], ids.take())
    a = a.reshape((ns, -1, half))
    b = b.reshape((nf, -1, width))
    a, b = multi_sum([a, b], "seq", [(ns, ss), (nf, sf)], ids.take())
    return jnp.concatenate([a, b], axis=1)


class Ids:
    def __init__(self):
        self.next = 0

    def take(self):
        self.next += 1
        return self.next - 1


def exchange(x, axis, n, stride, gather, cid, absolute=False):
    slots = n if absolute and gather else n - 1
    shape = (slots,) + (x.shape if gather else x.shape[1:])
    return pl.pallas_call(
        functools.partial(exchange_kernel, axis, n, stride, gather, absolute),
        out_shape=jax.ShapeDtypeStruct(shape, x.dtype),
        in_specs=[pl.BlockSpec(memory_space=pl.ANY)],
        out_specs=pl.BlockSpec(memory_space=pl.ANY),
        scratch_shapes=[
            pltpu.SemaphoreType.DMA((n - 1,)),
            pltpu.SemaphoreType.DMA((slots,)),
        ],
        compiler_params=pltpu.CompilerParams(collective_id=cid, has_side_effects=True),
    )(x)


def gather_rows(x, axis, digits, ids):
    for n, stride in digits:
        x = jnp.concatenate([x[None], exchange(x, axis, n, stride, True, ids.take())])
    return x.reshape((-1,) + x.shape[-1:])


def sum_scatter_rows(x, axis, digits, ids):
    for n, stride in reversed(digits):
        x = x.reshape((n, -1) + x.shape[-1:])
        x = x[0] + jnp.sum(exchange(x, axis, n, stride, False, ids.take()), axis=0)
    return x


def digit(axis, n, stride):
    return lax.rem(lax.axis_index(axis) // stride, n)


def gather_rows_absolute(x, axis, digits, ids):
    for n, stride in digits:
        y = exchange(x, axis, n, stride, True, ids.take(), absolute=True)
        x = lax.dynamic_update_index_in_dim(y, x, digit(axis, n, stride), 0)
    return x.reshape((-1,) + x.shape[-1:])


def sum_scatter_rows_absolute(x, axis, digits, ids):
    for n, stride in reversed(digits):
        x = x.reshape((n, -1) + x.shape[-1:])
        own = lax.dynamic_index_in_dim(x, digit(axis, n, stride), 0, keepdims=False)
        x = own + jnp.sum(exchange(x, axis, n, stride, False, ids.take(), absolute=True), axis=0)
    return x


def reorder_blocks(x, sizes):
    k = len(sizes)
    x = x.reshape(tuple(sizes) + (-1, x.shape[-1]))
    x = jnp.transpose(x, tuple(reversed(range(k))) + (k, k + 1))
    return x.reshape((-1, x.shape[-1]))


def seq_sum_scatter(x, digits, ids):
    x = reorder_blocks(x, [n for n, _ in digits])
    return sum_scatter_rows_absolute(x, "seq", digits, ids)


def seq_gather(x, digits, ids):
    x = gather_rows_absolute(x, "seq", digits, ids)
    return reorder_blocks(x, [n for n, _ in reversed(digits)])


def apply_mask(w, mask):
    r, c = mask.shape
    blocks = w.reshape((r, w.shape[0] // r, c, w.shape[1] // c))
    return (blocks * mask.astype(w.dtype)[:, None, :, None]).reshape(w.shape)


def gating(summed, width):
    gate = summed[:, :width]
    up = summed[:, width:]
    sig = jax.nn.sigmoid(gate)
    act = gate * sig
    return (gate, up, sig, act)


def gate_up_grads(gate, up, sig, act, grad_hidden):
    dgate = (grad_hidden * up * sig * (1.0 + gate * (1.0 - sig))).astype(jnp.bfloat16)
    dup = (grad_hidden * act).astype(jnp.bfloat16)
    return jnp.concatenate([dgate, dup], axis=1)


def per_device(tensor_digits, seq_digits, tokens, w_gate, w_up, w_down, mask_gate, mask_up, mask_down, cotangent):
    width = w_gate.shape[1]
    feat = tokens.shape[1]
    joined = jnp.concatenate([apply_mask(w_gate, mask_gate), apply_mask(w_up, mask_up)], axis=1)
    down_w = apply_mask(w_down, mask_down)
    contract_first = (((0,), (0,)), ((), ()))
    contract_last = (((1,), (1,)), ((), ()))
    ids = Ids()
    cot_rows = gather_rows(cotangent, "tensor", tensor_digits, ids)
    grad_part = lax.dot_general(cot_rows, down_w, contract_last, preferred_element_type=jnp.float32)
    grad_part, tokens = lax.optimization_barrier((grad_part, tokens))
    grad_hidden = lax.psum_scatter(grad_part, "seq", scatter_dimension=0, tiled=True)
    gathered = gather_rows(tokens, "tensor", tensor_digits, ids)
    partial_value = jnp.dot(gathered, joined, preferred_element_type=jnp.float32)
    summed = seq_sum_scatter_2d(partial_value, seq_digits, ids)
    gate, up, sig, act = gating(summed, width)
    hidden_part = (act * up).astype(jnp.bfloat16)
    hidden = seq_gather(hidden_part, seq_digits, ids)
    output = sum_scatter_rows(
        jnp.dot(hidden, down_w, preferred_element_type=jnp.float32), "tensor", tensor_digits, ids
    ).astype(jnp.bfloat16)
    grads_part = gate_up_grads(gate, up, sig, act, grad_hidden)
    grads_part, hidden = lax.optimization_barrier((grads_part, hidden))
    grads = lax.all_gather(grads_part, "seq", axis=0, tiled=True)
    grad_tokens = sum_scatter_rows(
        lax.dot_general(grads, joined, contract_last, preferred_element_type=jnp.float32),
        "tensor",
        tensor_digits,
        ids,
    ).astype(jnp.bfloat16)
    weight_grad = lax.dot_general(
        gathered, grads, contract_first, preferred_element_type=jnp.float32
    )
    grad_gate = apply_mask(weight_grad[:, :width], mask_gate).astype(jnp.bfloat16)
    grad_up = apply_mask(weight_grad[:, width:], mask_up).astype(jnp.bfloat16)
    down_grad = lax.dot_general(
        hidden, cot_rows, contract_first, preferred_element_type=jnp.float32
    )
    grad_down = apply_mask(down_grad, mask_down).astype(jnp.bfloat16)
    return (output, grad_tokens, grad_gate, grad_up, grad_down)


def axis_parts(mesh, axis):
    n = mesh.shape[axis]
    line = np.moveaxis(mesh.devices, mesh.axis_names.index(axis), -1).reshape(-1, n)[0]
    try:
        keys = [tuple(d.coords) + (d.core_on_chip,) for d in line]
    except AttributeError:
        return [n]
    parts, stride = [], 1
    while stride < n:
        changed = [c for c in range(len(keys[0])) if keys[stride][c] != keys[0][c]]
        size = 1
        while stride * size < n:
            moved = [c for c in range(len(keys[0])) if keys[stride * size][c] != keys[0][c]]
            if moved != changed:
                break
            size += 1
        if (n // stride) % size:
            return [n]
        parts.append(size)
        stride *= size
    return parts[::-1]


def digits_of(mesh, axis):
    sizes = axis_parts(mesh, axis)
    digits, stride = [], 1
    for n in reversed(sizes):
        if n > 1:
            digits.append((n, stride))
        stride *= n
    return tuple(reversed(digits))


def solution(mesh):
    return jax.shard_map(
        functools.partial(per_device, digits_of(mesh, "tensor"), digits_of(mesh, "seq")),
        mesh=mesh,
        in_specs=(
            P("tensor", "seq"),
            P("seq", "tensor"),
            P("seq", "tensor"),
            P("tensor", "seq"),
            P("seq", "tensor"),
            P("seq", "tensor"),
            P("tensor", "seq"),
            P("tensor", "seq"),
        ),
        out_specs=(
            P("tensor", "seq"),
            P("tensor", "seq"),
            P("seq", "tensor"),
            P("seq", "tensor"),
            P("tensor", "seq"),
        ),
        check_vma=False,
    )
```

```python
import functools

import jax
import numpy as np
import jax.numpy as jnp
from jax import lax
from jax.experimental import pallas as pl
from jax.experimental.pallas import tpu as pltpu
from jax.sharding import PartitionSpec as P

MESH = pl.DeviceIdType.MESH
AXES = ("seq", "tensor")


def peer(axis, j):
    return tuple(j if a == axis else lax.axis_index(a) for a in AXES)


def exchange_kernel(axis, n, stride, gather, absolute, x_ref, y_ref, send_sem, recv_sem):
    index = lax.axis_index(axis)
    me = lax.rem(index // stride, n)
    base = index - me * stride
    barrier = pltpu.get_barrier_semaphore()

    def device(j):
        return peer(axis, base + j * stride)

    def greet(k, carry):
        pl.semaphore_signal(
            barrier, inc=1, device_id=device(lax.rem(me + k, n)), device_id_type=MESH
        )
        return carry

    lax.fori_loop(1, n, greet, 0)
    pl.semaphore_wait(barrier, n - 1)

    def remote(k, direction):
        other = lax.rem(me + direction * k + n, n)
        if absolute and gather:
            slot = me if direction == ahead else other
        else:
            slot = k - 1
        return pltpu.make_async_remote_copy(
            src_ref=x_ref if gather else x_ref.at[other if absolute else k],
            dst_ref=y_ref.at[slot],
            send_sem=send_sem.at[k - 1],
            recv_sem=recv_sem.at[slot],
            device_id=device(other),
            device_id_type=MESH,
        )

    ahead = 1 if absolute or not gather else -1

    def send(k, carry):
        remote(k, ahead).start()
        return carry

    lax.fori_loop(1, n, send, 0)

    def finish(k, carry):
        remote(k, ahead).wait_send()
        remote(k, -ahead).wait_recv()
        return carry

    lax.fori_loop(1, n, finish, 0)


def multi_sum_kernel(axis, groups, gather, *refs):
    m = len(groups)
    x_refs, y_refs, sems = refs[:m], refs[m:2 * m], refs[2 * m:]
    index = lax.axis_index(axis)
    barrier = pltpu.get_barrier_semaphore()
    infos = []
    for n, stride in groups:
        me = lax.rem(index // stride, n)
        infos.append((n, stride, me, index - me * stride))
    for n, stride, me, base in infos:

        def greet(k, carry, n=n, stride=stride, me=me, base=base):
            j = lax.rem(me + k, n)
            pl.semaphore_signal(
                barrier, inc=1, device_id=peer(axis, base + j * stride), device_id_type=MESH
            )
            return carry

        lax.fori_loop(1, n, greet, 0)
    pl.semaphore_wait(barrier, sum(n - 1 for n, _ in groups))

    def remote(g, k, direction):
        n, stride, me, base = infos[g]
        other = lax.rem(me + direction * k + n, n)
        if gather:
            slot = me if direction == 1 else other
        else:
            slot = k - 1
        return pltpu.make_async_remote_copy(
            src_ref=x_refs[g] if gather else x_refs[g].at[other],
            dst_ref=y_refs[g].at[slot],
            send_sem=sems[2 * g].at[k - 1],
            recv_sem=sems[2 * g + 1].at[slot],
            device_id=peer(axis, base + other * stride),
            device_id_type=MESH,
        )

    for g in range(m):

        def send(k, carry, g=g):
            remote(g, k, 1).start()
            return carry

        lax.fori_loop(1, groups[g][0], send, 0)
    for g in range(m):

        def finish(k, carry, g=g):
            remote(g, k, 1).wait_send()
            remote(g, k, -1).wait_recv()
            return carry

        lax.fori_loop(1, groups[g][0], finish, 0)


def multi_call(xs, axis, groups, cid, gather):
    sems = []
    for n, _ in groups:
        sems += [pltpu.SemaphoreType.DMA((n - 1,)), pltpu.SemaphoreType.DMA((n if gather else n - 1,))]
    shapes = [(n,) + x.shape if gather else (n - 1,) + x.shape[1:] for x, (n, _) in zip(xs, groups)]
    return pl.pallas_call(
        functools.partial(multi_sum_kernel, axis, tuple(groups), gather),
        out_shape=[jax.ShapeDtypeStruct(shape, x.dtype) for x, shape in zip(xs, shapes)],
        in_specs=[pl.BlockSpec(memory_space=pl.ANY)] * len(xs),
        out_specs=[pl.BlockSpec(memory_space=pl.ANY)] * len(xs),
        scratch_shapes=sems,
        compiler_params=pltpu.CompilerParams(collective_id=cid, has_side_effects=True),
    )(*xs)


def multi_gather(xs, axis, groups, cid):
    ys = multi_call(xs, axis, groups, cid, True)
    return [
        lax.dynamic_update_index_in_dim(y, x, digit(axis, n, stride), 0)
        for x, y, (n, stride) in zip(xs, ys, groups)
    ]


def multi_sum(xs, axis, groups, cid):
    ys = multi_call(xs, axis, groups, cid, False)
    out = []
    for x, y, (n, stride) in zip(xs, ys, groups):
        own = lax.dynamic_index_in_dim(x, digit(axis, n, stride), 0, keepdims=False)
        out.append(own + jnp.sum(y, axis=0))
    return out


def seq_gather_2d(x, digits, ids):
    if len(digits) != 2:
        return seq_gather(x, digits, ids)
    (ns, ss), (nf, sf) = digits
    half = x.shape[1] // 2
    a, b = multi_gather([x[:, :half], x[:, half:]], "seq", [(ns, ss), (nf, sf)], ids.take())
    a, b = multi_gather([a, b], "seq", [(nf, sf), (ns, ss)], ids.take())
    a = jnp.swapaxes(a, 0, 1).reshape((-1, half))
    b = b.reshape((-1, b.shape[-1]))
    return jnp.concatenate([a, b], axis=1)


def seq_sum_scatter_2d(x, digits, ids):
    if len(digits) != 2:
        return lax.psum_scatter(x, "seq", scatter_dimension=0, tiled=True)
    (ns, ss), (nf, sf) = digits
    half = x.shape[1] // 2
    width = x.shape[1] - half
    a = reorder_blocks(x[:, :half], [ns, nf]).reshape((nf, -1, half))
    b = x[:, half:].reshape((ns, -1, width))
    a, b = multi_sum([a, b], "seq", [(nf, sf), (ns, ss)], ids.take())
    a = a.reshape((ns, -1, half))
    b = b.reshape((nf, -1, width))
    a, b = multi_sum([a, b], "seq", [(ns, ss), (nf, sf)], ids.take())
    return jnp.concatenate([a, b], axis=1)


class Ids:
    def __init__(self):
        self.next = 0

    def take(self):
        self.next += 1
        return self.next - 1


def exchange(x, axis, n, stride, gather, cid, absolute=False):
    slots = n if absolute and gather else n - 1
    shape = (slots,) + (x.shape if gather else x.shape[1:])
    return pl.pallas_call(
        functools.partial(exchange_kernel, axis, n, stride, gather, absolute),
        out_shape=jax.ShapeDtypeStruct(shape, x.dtype),
        in_specs=[pl.BlockSpec(memory_space=pl.ANY)],
        out_specs=pl.BlockSpec(memory_space=pl.ANY),
        scratch_shapes=[
            pltpu.SemaphoreType.DMA((n - 1,)),
            pltpu.SemaphoreType.DMA((slots,)),
        ],
        compiler_params=pltpu.CompilerParams(collective_id=cid, has_side_effects=True),
    )(x)


def gather_rows(x, axis, digits, ids):
    for n, stride in digits:
        x = jnp.concatenate([x[None], exchange(x, axis, n, stride, True, ids.take())])
    return x.reshape((-1,) + x.shape[-1:])


def sum_scatter_rows(x, axis, digits, ids):
    for n, stride in reversed(digits):
        x = x.reshape((n, -1) + x.shape[-1:])
        x = x[0] + jnp.sum(exchange(x, axis, n, stride, False, ids.take()), axis=0)
    return x


def digit(axis, n, stride):
    return lax.rem(lax.axis_index(axis) // stride, n)


def gather_rows_absolute(x, axis, digits, ids):
    for n, stride in digits:
        y = exchange(x, axis, n, stride, True, ids.take(), absolute=True)
        x = lax.dynamic_update_index_in_dim(y, x, digit(axis, n, stride), 0)
    return x.reshape((-1,) + x.shape[-1:])


def sum_scatter_rows_absolute(x, axis, digits, ids):
    for n, stride in reversed(digits):
        x = x.reshape((n, -1) + x.shape[-1:])
        own = lax.dynamic_index_in_dim(x, digit(axis, n, stride), 0, keepdims=False)
        x = own + jnp.sum(exchange(x, axis, n, stride, False, ids.take(), absolute=True), axis=0)
    return x


def reorder_blocks(x, sizes):
    k = len(sizes)
    x = x.reshape(tuple(sizes) + (-1, x.shape[-1]))
    x = jnp.transpose(x, tuple(reversed(range(k))) + (k, k + 1))
    return x.reshape((-1, x.shape[-1]))


def seq_sum_scatter(x, digits, ids):
    x = reorder_blocks(x, [n for n, _ in digits])
    return sum_scatter_rows_absolute(x, "seq", digits, ids)


def seq_gather(x, digits, ids):
    x = gather_rows_absolute(x, "seq", digits, ids)
    return reorder_blocks(x, [n for n, _ in reversed(digits)])


def widen(mask, rows):
    block = rows // mask.shape[0]
    full = jnp.repeat(jnp.repeat(mask, block, axis=0), block, axis=1)
    return full.astype(jnp.bfloat16)


def gating(summed, width):
    gate = summed[:, :width]
    up = summed[:, width:]
    sig = jax.nn.sigmoid(gate)
    act = gate * sig
    return (gate, up, sig, act)


def gate_up_grads(gate, up, sig, act, grad_hidden):
    dgate = (grad_hidden * up * sig * (1.0 + gate * (1.0 - sig))).astype(jnp.bfloat16)
    dup = (grad_hidden * act).astype(jnp.bfloat16)
    return jnp.concatenate([dgate, dup], axis=1)


def per_device(tensor_digits, seq_digits, tokens, w_gate, w_up, w_down, mask_gate, mask_up, mask_down, cotangent):
    width = w_gate.shape[1]
    feat = tokens.shape[1]
    gate_mask = widen(mask_gate, w_gate.shape[0])
    up_mask = widen(mask_up, w_up.shape[0])
    down_mask = widen(mask_down, w_down.shape[0])
    joined = jnp.concatenate([w_gate * gate_mask, w_up * up_mask], axis=1)
    down_w = w_down * down_mask
    contract_first = (((0,), (0,)), ((), ()))
    contract_last = (((1,), (1,)), ((), ()))
    ids = Ids()
    cot_rows = gather_rows(cotangent, "tensor", tensor_digits, ids)
    grad_part = lax.dot_general(cot_rows, down_w, contract_last, preferred_element_type=jnp.float32)
    grad_part, tokens = lax.optimization_barrier((grad_part, tokens))
    grad_hidden = lax.psum_scatter(grad_part, "seq", scatter_dimension=0, tiled=True)
    gathered = gather_rows(tokens, "tensor", tensor_digits, ids)
    partial_value = jnp.dot(gathered, joined, preferred_element_type=jnp.float32)
    summed = seq_sum_scatter_2d(partial_value, seq_digits, ids)
    gate, up, sig, act = gating(summed, width)
    hidden_part = (act * up).astype(jnp.bfloat16)
    hidden = seq_gather_2d(hidden_part, seq_digits, ids)
    output = sum_scatter_rows(
        jnp.dot(hidden, down_w, preferred_element_type=jnp.float32), "tensor", tensor_digits, ids
    ).astype(jnp.bfloat16)
    grads_part = gate_up_grads(gate, up, sig, act, grad_hidden)
    grads_part, hidden = lax.optimization_barrier((grads_part, hidden))
    grads = lax.all_gather(grads_part, "seq", axis=0, tiled=True)
    grad_tokens = sum_scatter_rows(
        lax.dot_general(grads, joined, contract_last, preferred_element_type=jnp.float32),
        "tensor",
        tensor_digits,
        ids,
    ).astype(jnp.bfloat16)
    weight_grad = lax.dot_general(
        gathered, grads, contract_first, preferred_element_type=jnp.float32
    )
    grad_gate = (weight_grad[:, :width] * gate_mask).astype(jnp.bfloat16)
    grad_up = (weight_grad[:, width:] * up_mask).astype(jnp.bfloat16)
    down_grad = lax.dot_general(
        hidden, cot_rows, contract_first, preferred_element_type=jnp.float32
    )
    grad_down = (down_grad * down_mask).astype(jnp.bfloat16)
    return (output, grad_tokens, grad_gate, grad_up, grad_down)


def axis_parts(mesh, axis):
    n = mesh.shape[axis]
    line = np.moveaxis(mesh.devices, mesh.axis_names.index(axis), -1).reshape(-1, n)[0]
    try:
        keys = [tuple(d.coords) + (d.core_on_chip,) for d in line]
    except AttributeError:
        return [n]
    parts, stride = [], 1
    while stride < n:
        changed = [c for c in range(len(keys[0])) if keys[stride][c] != keys[0][c]]
        size = 1
        while stride * size < n:
            moved = [c for c in range(len(keys[0])) if keys[stride * size][c] != keys[0][c]]
            if moved != changed:
                break
            size += 1
        if (n // stride) % size:
            return [n]
        parts.append(size)
        stride *= size
    return parts[::-1]


def digits_of(mesh, axis):
    sizes = axis_parts(mesh, axis)
    digits, stride = [], 1
    for n in reversed(sizes):
        if n > 1:
            digits.append((n, stride))
        stride *= n
    return tuple(reversed(digits))


def solution(mesh):
    return jax.shard_map(
        functools.partial(per_device, digits_of(mesh, "tensor"), digits_of(mesh, "seq")),
        mesh=mesh,
        in_specs=(
            P("tensor", "seq"),
            P("seq", "tensor"),
            P("seq", "tensor"),
            P("tensor", "seq"),
            P("seq", "tensor"),
            P("seq", "tensor"),
            P("tensor", "seq"),
            P("tensor", "seq"),
        ),
        out_specs=(
            P("tensor", "seq"),
            P("tensor", "seq"),
            P("seq", "tensor"),
            P("seq", "tensor"),
            P("tensor", "seq"),
        ),
        check_vma=False,
    )
```

```python
import functools

import jax
import numpy as np
import jax.numpy as jnp
from jax import lax
from jax.experimental import pallas as pl
from jax.experimental.pallas import tpu as pltpu
from jax.sharding import PartitionSpec as P

MESH = pl.DeviceIdType.MESH
AXES = ("seq", "tensor")


def peer(axis, j):
    return tuple(j if a == axis else lax.axis_index(a) for a in AXES)


def exchange_kernel(axis, n, stride, gather, absolute, x_ref, y_ref, send_sem, recv_sem):
    index = lax.axis_index(axis)
    me = lax.rem(index // stride, n)
    base = index - me * stride
    barrier = pltpu.get_barrier_semaphore()

    def device(j):
        return peer(axis, base + j * stride)

    def greet(k, carry):
        pl.semaphore_signal(
            barrier, inc=1, device_id=device(lax.rem(me + k, n)), device_id_type=MESH
        )
        return carry

    lax.fori_loop(1, n, greet, 0)
    pl.semaphore_wait(barrier, n - 1)

    def remote(k, direction):
        other = lax.rem(me + direction * k + n, n)
        if absolute and gather:
            slot = me if direction == ahead else other
        else:
            slot = k - 1
        return pltpu.make_async_remote_copy(
            src_ref=x_ref if gather else x_ref.at[other if absolute else k],
            dst_ref=y_ref.at[slot],
            send_sem=send_sem.at[k - 1],
            recv_sem=recv_sem.at[slot],
            device_id=device(other),
            device_id_type=MESH,
        )

    ahead = 1 if absolute or not gather else -1

    def send(k, carry):
        remote(k, ahead).start()
        return carry

    lax.fori_loop(1, n, send, 0)

    def finish(k, carry):
        remote(k, ahead).wait_send()
        remote(k, -ahead).wait_recv()
        return carry

    lax.fori_loop(1, n, finish, 0)


def multi_sum_kernel(axis, groups, gather, *refs):
    m = len(groups)
    x_refs, y_refs, sems = refs[:m], refs[m:2 * m], refs[2 * m:]
    index = lax.axis_index(axis)
    barrier = pltpu.get_barrier_semaphore()
    infos = []
    for n, stride in groups:
        me = lax.rem(index // stride, n)
        infos.append((n, stride, me, index - me * stride))
    for n, stride, me, base in infos:

        def greet(k, carry, n=n, stride=stride, me=me, base=base):
            j = lax.rem(me + k, n)
            pl.semaphore_signal(
                barrier, inc=1, device_id=peer(axis, base + j * stride), device_id_type=MESH
            )
            return carry

        lax.fori_loop(1, n, greet, 0)
    pl.semaphore_wait(barrier, sum(n - 1 for n, _ in groups))

    def remote(g, k, direction):
        n, stride, me, base = infos[g]
        other = lax.rem(me + direction * k + n, n)
        if gather:
            slot = me if direction == 1 else other
        else:
            slot = k - 1
        return pltpu.make_async_remote_copy(
            src_ref=x_refs[g] if gather else x_refs[g].at[other],
            dst_ref=y_refs[g].at[slot],
            send_sem=sems[2 * g].at[k - 1],
            recv_sem=sems[2 * g + 1].at[slot],
            device_id=peer(axis, base + other * stride),
            device_id_type=MESH,
        )

    for g in range(m):

        def send(k, carry, g=g):
            remote(g, k, 1).start()
            return carry

        lax.fori_loop(1, groups[g][0], send, 0)
    for g in range(m):

        def finish(k, carry, g=g):
            remote(g, k, 1).wait_send()
            remote(g, k, -1).wait_recv()
            return carry

        lax.fori_loop(1, groups[g][0], finish, 0)


def multi_call(xs, axis, groups, cid, gather):
    sems = []
    for n, _ in groups:
        sems += [pltpu.SemaphoreType.DMA((n - 1,)), pltpu.SemaphoreType.DMA((n if gather else n - 1,))]
    shapes = [(n,) + x.shape if gather else (n - 1,) + x.shape[1:] for x, (n, _) in zip(xs, groups)]
    return pl.pallas_call(
        functools.partial(multi_sum_kernel, axis, tuple(groups), gather),
        out_shape=[jax.ShapeDtypeStruct(shape, x.dtype) for x, shape in zip(xs, shapes)],
        in_specs=[pl.BlockSpec(memory_space=pl.ANY)] * len(xs),
        out_specs=[pl.BlockSpec(memory_space=pl.ANY)] * len(xs),
        scratch_shapes=sems,
        compiler_params=pltpu.CompilerParams(collective_id=cid, has_side_effects=True),
    )(*xs)


def multi_gather(xs, axis, groups, cid):
    ys = multi_call(xs, axis, groups, cid, True)
    return [
        lax.dynamic_update_index_in_dim(y, x, digit(axis, n, stride), 0)
        for x, y, (n, stride) in zip(xs, ys, groups)
    ]


def multi_sum(xs, axis, groups, cid):
    ys = multi_call(xs, axis, groups, cid, False)
    out = []
    for x, y, (n, stride) in zip(xs, ys, groups):
        own = lax.dynamic_index_in_dim(x, digit(axis, n, stride), 0, keepdims=False)
        out.append(own + jnp.sum(y, axis=0))
    return out


def seq_gather_2d(x, digits, ids):
    half = x.shape[1] // 2
    if len(digits) != 2:
        x = seq_gather(x, digits, ids)
        return [x[:, :half], x[:, half:]]
    (ns, ss), (nf, sf) = digits
    a, b = multi_gather([x[:, :half], x[:, half:]], "seq", [(ns, ss), (nf, sf)], ids.take())
    a, b = multi_gather([a, b], "seq", [(nf, sf), (ns, ss)], ids.take())
    a = jnp.swapaxes(a, 0, 1).reshape((-1, half))
    b = b.reshape((-1, b.shape[-1]))
    return [a, b]


def seq_sum_scatter_2d(x, digits, ids):
    if len(digits) != 2:
        return lax.psum_scatter(x, "seq", scatter_dimension=0, tiled=True)
    (ns, ss), (nf, sf) = digits
    half = x.shape[1] // 2
    width = x.shape[1] - half
    a = reorder_blocks(x[:, :half], [ns, nf]).reshape((nf, -1, half))
    b = x[:, half:].reshape((ns, -1, width))
    a, b = multi_sum([a, b], "seq", [(nf, sf), (ns, ss)], ids.take())
    a = a.reshape((ns, -1, half))
    b = b.reshape((nf, -1, width))
    a, b = multi_sum([a, b], "seq", [(ns, ss), (nf, sf)], ids.take())
    return jnp.concatenate([a, b], axis=1)


class Ids:
    def __init__(self):
        self.next = 0

    def take(self):
        self.next += 1
        return self.next - 1


def exchange(x, axis, n, stride, gather, cid, absolute=False):
    slots = n if absolute and gather else n - 1
    shape = (slots,) + (x.shape if gather else x.shape[1:])
    return pl.pallas_call(
        functools.partial(exchange_kernel, axis, n, stride, gather, absolute),
        out_shape=jax.ShapeDtypeStruct(shape, x.dtype),
        in_specs=[pl.BlockSpec(memory_space=pl.ANY)],
        out_specs=pl.BlockSpec(memory_space=pl.ANY),
        scratch_shapes=[
            pltpu.SemaphoreType.DMA((n - 1,)),
            pltpu.SemaphoreType.DMA((slots,)),
        ],
        compiler_params=pltpu.CompilerParams(collective_id=cid, has_side_effects=True),
    )(x)


def gather_rows(x, axis, digits, ids):
    for n, stride in digits:
        x = jnp.concatenate([x[None], exchange(x, axis, n, stride, True, ids.take())])
    return x.reshape((-1,) + x.shape[-1:])


def sum_scatter_rows(x, axis, digits, ids):
    for n, stride in reversed(digits):
        x = x.reshape((n, -1) + x.shape[-1:])
        x = x[0] + jnp.sum(exchange(x, axis, n, stride, False, ids.take()), axis=0)
    return x


def digit(axis, n, stride):
    return lax.rem(lax.axis_index(axis) // stride, n)


def gather_rows_absolute(x, axis, digits, ids):
    for n, stride in digits:
        y = exchange(x, axis, n, stride, True, ids.take(), absolute=True)
        x = lax.dynamic_update_index_in_dim(y, x, digit(axis, n, stride), 0)
    return x.reshape((-1,) + x.shape[-1:])


def sum_scatter_rows_absolute(x, axis, digits, ids):
    for n, stride in reversed(digits):
        x = x.reshape((n, -1) + x.shape[-1:])
        own = lax.dynamic_index_in_dim(x, digit(axis, n, stride), 0, keepdims=False)
        x = own + jnp.sum(exchange(x, axis, n, stride, False, ids.take(), absolute=True), axis=0)
    return x


def reorder_blocks(x, sizes):
    k = len(sizes)
    x = x.reshape(tuple(sizes) + (-1, x.shape[-1]))
    x = jnp.transpose(x, tuple(reversed(range(k))) + (k, k + 1))
    return x.reshape((-1, x.shape[-1]))


def seq_sum_scatter(x, digits, ids):
    x = reorder_blocks(x, [n for n, _ in digits])
    return sum_scatter_rows_absolute(x, "seq", digits, ids)


def seq_gather(x, digits, ids):
    x = gather_rows_absolute(x, "seq", digits, ids)
    return reorder_blocks(x, [n for n, _ in reversed(digits)])


def widen(mask, rows):
    block = rows // mask.shape[0]
    full = jnp.repeat(jnp.repeat(mask, block, axis=0), block, axis=1)
    return full.astype(jnp.bfloat16)


def gating(summed, width):
    gate = summed[:, :width]
    up = summed[:, width:]
    sig = jax.nn.sigmoid(gate)
    act = gate * sig
    return (gate, up, sig, act)


def gate_up_grads(gate, up, sig, act, grad_hidden):
    dgate = (grad_hidden * up * sig * (1.0 + gate * (1.0 - sig))).astype(jnp.bfloat16)
    dup = (grad_hidden * act).astype(jnp.bfloat16)
    return jnp.concatenate([dgate, dup], axis=1)


def per_device(tensor_digits, seq_digits, tokens, w_gate, w_up, w_down, mask_gate, mask_up, mask_down, cotangent):
    width = w_gate.shape[1]
    feat = tokens.shape[1]
    gate_mask = widen(mask_gate, w_gate.shape[0])
    up_mask = widen(mask_up, w_up.shape[0])
    down_mask = widen(mask_down, w_down.shape[0])
    joined = jnp.concatenate([w_gate * gate_mask, w_up * up_mask], axis=1)
    down_w = w_down * down_mask
    contract_first = (((0,), (0,)), ((), ()))
    contract_last = (((1,), (1,)), ((), ()))
    ids = Ids()
    cot_rows = gather_rows(cotangent, "tensor", tensor_digits, ids)
    grad_part = lax.dot_general(cot_rows, down_w, contract_last, preferred_element_type=jnp.float32)
    grad_part, tokens = lax.optimization_barrier((grad_part, tokens))
    grad_hidden = lax.psum_scatter(grad_part, "seq", scatter_dimension=0, tiled=True)
    gathered = gather_rows(tokens, "tensor", tensor_digits, ids)
    partial_value = jnp.dot(gathered, joined, preferred_element_type=jnp.float32)
    summed = seq_sum_scatter_2d(partial_value, seq_digits, ids)
    gate, up, sig, act = gating(summed, width)
    hidden_part = (act * up).astype(jnp.bfloat16)
    hidden = seq_gather_2d(hidden_part, seq_digits, ids)
    cut = hidden[0].shape[1]
    output_part = jnp.dot(hidden[0], down_w[:cut], preferred_element_type=jnp.float32) + jnp.dot(
        hidden[1], down_w[cut:], preferred_element_type=jnp.float32
    )
    output = sum_scatter_rows(output_part, "tensor", tensor_digits, ids).astype(jnp.bfloat16)
    grads_part = gate_up_grads(gate, up, sig, act, grad_hidden)
    grads_part, hidden = lax.optimization_barrier((grads_part, hidden))
    grads = lax.all_gather(grads_part, "seq", axis=0, tiled=True)
    grad_tokens = sum_scatter_rows(
        lax.dot_general(grads, joined, contract_last, preferred_element_type=jnp.float32),
        "tensor",
        tensor_digits,
        ids,
    ).astype(jnp.bfloat16)
    weight_grad = lax.dot_general(
        gathered, grads, contract_first, preferred_element_type=jnp.float32
    )
    grad_gate = (weight_grad[:, :width] * gate_mask).astype(jnp.bfloat16)
    grad_up = (weight_grad[:, width:] * up_mask).astype(jnp.bfloat16)
    down_grad = jnp.concatenate(
        [
            lax.dot_general(piece, cot_rows, contract_first, preferred_element_type=jnp.float32)
            for piece in hidden
        ]
    )
    grad_down = (down_grad * down_mask).astype(jnp.bfloat16)
    return (output, grad_tokens, grad_gate, grad_up, grad_down)


def axis_parts(mesh, axis):
    n = mesh.shape[axis]
    line = np.moveaxis(mesh.devices, mesh.axis_names.index(axis), -1).reshape(-1, n)[0]
    try:
        keys = [tuple(d.coords) + (d.core_on_chip,) for d in line]
    except AttributeError:
        return [n]
    parts, stride = [], 1
    while stride < n:
        changed = [c for c in range(len(keys[0])) if keys[stride][c] != keys[0][c]]
        size = 1
        while stride * size < n:
            moved = [c for c in range(len(keys[0])) if keys[stride * size][c] != keys[0][c]]
            if moved != changed:
                break
            size += 1
        if (n // stride) % size:
            return [n]
        parts.append(size)
        stride *= size
    return parts[::-1]


def digits_of(mesh, axis):
    sizes = axis_parts(mesh, axis)
    digits, stride = [], 1
    for n in reversed(sizes):
        if n > 1:
            digits.append((n, stride))
        stride *= n
    return tuple(reversed(digits))


def solution(mesh):
    return jax.shard_map(
        functools.partial(per_device, digits_of(mesh, "tensor"), digits_of(mesh, "seq")),
        mesh=mesh,
        in_specs=(
            P("tensor", "seq"),
            P("seq", "tensor"),
            P("seq", "tensor"),
            P("tensor", "seq"),
            P("seq", "tensor"),
            P("seq", "tensor"),
            P("tensor", "seq"),
            P("tensor", "seq"),
        ),
        out_specs=(
            P("tensor", "seq"),
            P("tensor", "seq"),
            P("seq", "tensor"),
            P("seq", "tensor"),
            P("tensor", "seq"),
        ),
        check_vma=False,
    )
```
